256 devices in a mesh: wide: 16 (over x_lo, y, core), narrow: 16 (over z, x_hi).
Axes of the slice: x: 4 (x_hi: 2, x_lo: 2; x = x_hi * 2 + x_lo), y: 4, z: 8, core: 2. Of those that a mesh axis runs over, the one named last changes fastest.
Arguments:
- coarse_basis: bfloat16 [32, 96, 3, 64, 8, 128], P('wide', None, None, 'narrow')
- material_ids: int32 [32, 64, 8, 128], P('wide', 'narrow'), may hold values from 0 to 15
- lame_table: bfloat16 [2, 16], replicated, may hold values from 0.5 to 4
- coarse_ids: int32 [32, 96], P('wide'), may hold values from 0 to 127, as said below
- coarse_slab: bfloat16 [98304, 2048], P('wide', 'narrow'), may hold values from -0.5 to 2.5, as said below
- panel_owner: int32 [1], replicated, may hold values from 0 to 14
Outputs:
- factored: bfloat16 [98304, 2048], P('wide', 'narrow')
- galerkin: float32 [32, 96, 96], P('wide')
The draws below stay inside these ranges and needn't reach their ends.
Inputs may be any that keep to these rules, and one draw needn't show every extreme that they name: `coarse_ids`: the 96 numbers of a row are distinct. `coarse_slab`: for every column block t, the 128 x 128 block whose rows begin at t * 6144 is symmetric positive definite.
All inputs are finite; a program needn't handle non-finite values.
Results may differ from the reference program's by a relative error of at most 0.001.
The reference program's roundings to bfloat16 on the way (of `factor`) count: a program that leaves them out, or rounds other values in their place, can miss the bound.
Values may be sent and summed in bfloat16 or wider, within the bound.
A program may use at most 192 MiB of HBM per device.

```python
import math
import jax
import jax.numpy as jnp
from jax import lax

NG = 98304
NFN = 96
CB = 128
CZ = 128
NMAT = 16
SUB_W = 2
CY = 8
NXS = 64
SUBS = 32
ROWS_W = 6144
STRIDE = 1
NW = 2048
OWNER_SPAN = 15


def draw_coarse_basis(key, part):
    base_key = jax.random.fold_in(jax.random.fold_in(key, 11), 0)
    field_key = jax.random.fold_in(jax.random.fold_in(key, 11), 2)
    mix_key = jax.random.fold_in(jax.random.fold_in(key, 11), 3)
    shape = (SUBS, NFN, 3, NXS, CY, CZ)
    field_shape = (6, SUBS, 3, NXS, CY, CZ)
    raw = jax.random.truncated_normal(base_key, -4.0, 4.0, shape, jnp.float32)
    shared = jax.random.truncated_normal(field_key, -4.0, 4.0, field_shape, jnp.float32)
    mixing = 0.6 * jax.random.truncated_normal(mix_key, -3.0, 3.0, (SUBS, NFN, 6), jnp.float32)
    mixed = raw
    for common in range(6):
        weight_now = mixing[:, :, common].reshape(SUBS, NFN, 1, 1, 1, 1)
        mixed = mixed + weight_now * shared[common][:, None]
    factor = (0.1 / (3.0 * NXS * CY * CZ)) ** 0.5
    return (mixed * factor).astype(jnp.bfloat16)


def one_order(order_key):
    return jax.random.permutation(order_key, CB)


def draw_coarse_ids(key, part):
    keys = jax.random.split(jax.random.fold_in(key, 23), SUBS)
    orders = jax.vmap(one_order)(keys)
    return orders[:, :NFN].astype(jnp.int32)


def draw_coarse_slab(key, part):
    entry_key, spread_key = jax.random.split(jax.random.fold_in(key, 37))
    loose = jax.random.uniform(entry_key, (NG, NW), jnp.float32, -0.5, 0.5)
    spread = jnp.exp(jax.random.uniform(spread_key, (NW // CB, CB), jnp.float32, -0.6931, 0.6931))
    distance = jnp.abs(jnp.arange(CB)[:, None] - jnp.arange(CB)[None, :]).astype(jnp.float32)
    kernel = jnp.power(0.88, distance)
    result = loose
    for column_block in range(NW // CB):
        first_row = column_block * STRIDE * ROWS_W
        scales = spread[column_block]
        tile = jnp.sqrt(scales[:, None] * scales[None, :]) * kernel + 0.5 * jnp.eye(CB, dtype=jnp.float32)
        result = result.at[first_row:first_row + CB, column_block * CB:(column_block + 1) * CB].set(tile)
    return result.astype(jnp.bfloat16)


def touch_ends(values, own_key, smallest, top_value):
    place = [jax.random.randint(jax.random.fold_in(own_key, axis), (), 0, length) for axis, length in enumerate(values.shape)]
    main_axis = values.shape.index(max(values.shape))
    neighbour = place[:main_axis] + [(place[main_axis] + 1) % values.shape[main_axis]] + place[main_axis + 1:]
    return values.at[tuple(place)].set(smallest).at[tuple(neighbour)].set(top_value)


def setup_inputs(seed: int = 0) -> dict:
    arg_keys = jax.random.split(jax.random.key(seed), 7)
    coarse_basis = draw_coarse_basis(jax.random.fold_in(arg_keys[6], 71), 0)
    material_ids = touch_ends(jax.random.randint(arg_keys[1], (SUBS, NXS, CY, CZ), 0, NMAT), jax.random.fold_in(arg_keys[1], 1), 0, NMAT - 1).astype(jnp.int32)
    lame_table = jnp.clip(jnp.exp(jax.random.uniform(arg_keys[2], (2, NMAT), jnp.float32, math.log(0.5), math.log(4.0))), 0.5, 4.0).astype(jnp.bfloat16)
    coarse_ids = draw_coarse_ids(jax.random.fold_in(arg_keys[6], 71), 0)
    coarse_slab = draw_coarse_slab(jax.random.fold_in(arg_keys[6], 71), 0)
    panel_owner = jax.random.randint(arg_keys[5], (1,), 0, OWNER_SPAN).astype(jnp.int32)
    return {"coarse_basis": coarse_basis, "material_ids": material_ids, "lame_table": lame_table, "coarse_ids": coarse_ids, "coarse_slab": coarse_slab, "panel_owner": panel_owner}


def lower_inverse(lower):
    identity = jnp.eye(lower.shape[0], dtype=lower.dtype)
    return lax.linalg.triangular_solve(lower, identity, left_side=True, lower=True)

def lame_fields(material_ids, lame_table):
    values = lame_table.astype(jnp.float32)
    shear = jnp.zeros(material_ids.shape, jnp.float32)
    dilatation = jnp.zeros(material_ids.shape, jnp.float32)
    for material in range(values.shape[1]):
        chosen = material_ids == material
        shear = jnp.where(chosen, values[0, material], shear)
        dilatation = jnp.where(chosen, values[1, material], dilatation)
    return (shear, dilatation)

def shifted(field, axis, step):
    length = field.shape[axis]
    border = jnp.zeros_like(lax.slice_in_dim(field, 0, 1, axis=axis))
    if step > 0:
        return jnp.concatenate([lax.slice_in_dim(field, 1, length, axis=axis), border], axis=axis)
    return jnp.concatenate([border, lax.slice_in_dim(field, 0, length - 1, axis=axis)], axis=axis)

def face_weight(coeff_one, coeff_two, direction):
    shear = 0.5 * (coeff_one[:, 0:1] + coeff_two[:, 0:1])
    dilate = 0.5 * (coeff_one[:, 1:2] + coeff_two[:, 1:2])
    unit = (jnp.arange(3) == direction).astype(shear.dtype).reshape(1, 1, 3, 1, 1, 1)
    return shear + unit * (dilate + shear)

def operator_image(padded, coeff):
    centre = padded[:, :, :, 1:-1]
    coeff_centre = coeff[:, :, :, 1:-1]
    pairs = [(padded[:, :, :, 2:], coeff[:, :, :, 2:], 0), (padded[:, :, :, :-2], coeff[:, :, :, :-2], 0)]
    for axis, direction in ((4, 1), (5, 2)):
        for step in (1, -1):
            pairs.append((shifted(centre, axis, step), shifted(coeff_centre, axis, step), direction))
    image = jnp.zeros(centre.shape, centre.dtype)
    for other, other_coeff, direction in pairs:
        image = image + face_weight(coeff_centre, other_coeff, direction) * (centre - other)
    return image

def galerkin_of(left_field, right_field):
    subs, funcs = (left_field.shape[0], left_field.shape[1])
    return jnp.einsum('sak,sbk->sab', left_field.reshape(subs, funcs, -1), right_field.reshape(subs, funcs, -1), precision=lax.Precision.HIGHEST)

def one_subdomain(items):
    field, coeff = items
    widths = ((0, 0), (0, 0), (0, 0), (1, 1), (0, 0), (0, 0))
    padded = jnp.pad(field.astype(jnp.float32)[None], widths)
    coeff_padded = jnp.pad(coeff[None], widths)
    image = operator_image(padded, coeff_padded)
    return galerkin_of(padded[:, :, :, 1:-1], image)[0]

def reference(coarse_basis, material_ids, lame_table, coarse_ids, coarse_slab, panel_owner):
    shear, dilatation = lame_fields(material_ids, lame_table)
    coeff = jnp.stack([shear, dilatation], 1)[:, :, None]
    galerkin = lax.map(one_subdomain, (coarse_basis, coeff))
    owner = panel_owner[0].astype(jnp.int32)
    added_blocks = []
    for column_block in range(NW // CB):
        first_sub = column_block * STRIDE * SUB_W
        members = galerkin[first_sub:first_sub + SUB_W]
        slots = (coarse_ids[first_sub:first_sub + SUB_W][:, :, None] == jnp.arange(CB)[None, None, :]).astype(jnp.float32)
        spread = jnp.einsum('sab,sbc->sac', members, slots, precision=lax.Precision.HIGHEST)
        added_blocks.append(jnp.einsum('sar,sac->rc', slots, spread, precision=lax.Precision.HIGHEST))
    stacked = jnp.stack(added_blocks, 0)
    added_owner = lax.dynamic_index_in_dim(stacked, owner, 0, keepdims=False)
    start_row = (owner * STRIDE * ROWS_W).astype(jnp.int32)
    diagonal = lax.dynamic_slice(coarse_slab, (start_row, (owner * CB).astype(jnp.int32)), (CB, CB)).astype(jnp.float32)
    diagonal = diagonal + added_owner
    diagonal = 0.5 * (diagonal + diagonal.T)
    lower = jnp.linalg.cholesky(diagonal)
    inverse = lower_inverse(lower)
    column = lax.dynamic_slice_in_dim(coarse_slab, (owner * CB).astype(jnp.int32), CB, axis=1)
    solved = jnp.dot(column.astype(jnp.float32), inverse.T, precision=lax.Precision.HIGHEST)
    rows = lax.broadcasted_iota(jnp.int32, (NG, CB), 0)
    wide_of = rows // ROWS_W
    head = rows % ROWS_W < CB
    diagonal_rows = head & (wide_of == owner * STRIDE)
    earlier = head & (wide_of % STRIDE == 0) & (wide_of // STRIDE < owner)
    own_block = lax.dynamic_update_slice(jnp.zeros((NG, CB), jnp.float32), lower, (start_row, jnp.int32(0)))
    solved = jnp.where(diagonal_rows, own_block, solved)
    solved = jnp.where(earlier, 0.0, solved)
    factor = solved.astype(jnp.bfloat16)
    blocks = []
    for column_block in range(NW // CB):
        first_row = column_block * STRIDE * ROWS_W
        added = added_blocks[column_block]
        base = coarse_slab[:, column_block * CB:(column_block + 1) * CB].astype(jnp.float32)
        base = base.at[first_row:first_row + CB].add(jnp.where(column_block >= owner, added, 0.0))
        rows_needed = factor[first_row:first_row + CB]
        update = jnp.dot(factor.astype(jnp.float32), rows_needed.T.astype(jnp.float32), preferred_element_type=jnp.float32)
        result = jnp.where(column_block > owner, base - update, base)
        result = jnp.where(column_block == owner, factor.astype(jnp.float32), result)
        blocks.append(result.astype(jnp.bfloat16))
    return (jnp.concatenate(blocks, axis=1), galerkin)
```

```python
import functools

import jax
import jax.numpy as jnp
from jax import lax
from jax.experimental import pallas as pl
from jax.experimental.pallas import tpu as pltpu
from jax.sharding import PartitionSpec as P

MESH = pl.DeviceIdType.MESH
F32, BF16 = jnp.float32, jnp.bfloat16
NT = (((1,), (1,)), ((), ()))
NN = (((1,), (0,)), ((), ()))
PIECE = 24


def exact_dot(a, b, dims):
    return lax.dot_general(a, b, dims, precision=lax.Precision.HIGHEST, preferred_element_type=F32)


def split2(x):
    hi = x.astype(BF16)
    return hi, (x - hi.astype(F32)).astype(BF16)


def shift_up(x, axis):
    index = lax.broadcasted_iota(jnp.int32, x.shape, axis)
    return jnp.where(index == 0, 0.0, pltpu.roll(x, 1, axis))


def shift_down(x, axis):
    size = x.shape[axis]
    index = lax.broadcasted_iota(jnp.int32, x.shape, axis)
    return jnp.where(index == size - 1, 0.0, pltpu.roll(x, size - 1, axis))


def gather_kernel(
    owner_ref, table_ref, ids_ref, basis_ref, mat_ref, slab_ref,
    own_ref, panel_ref,
    tiles, halo, mats, mat_halo, head, coef, coef_halo, natural, left, right, first, acc, late,
    pieces, landed, reduced, wide_in, chosen,
    load_sem, small_sem, halo_send, halo_recv, mat_send, mat_recv, rs_send, rs_recv,
    wide_send, wide_recv, own_send, own_recv, panel_send, panel_recv,
):
    w, n = lax.axis_index("wide"), lax.axis_index("narrow")
    count = lax.axis_size("narrow")
    funcs = basis_ref.shape[1]
    layers = basis_ref.shape[3]
    group = lambda d: lax.rem(n + d, count)
    across = lambda d: lax.rem(w + d, count)

    def load(sc):
        s, c = lax.div(sc, 3), lax.rem(sc, 3)
        return pltpu.make_async_copy(basis_ref.at[s, :, c], tiles.at[sc], load_sem.at[sc])

    def halo_copy(sc):
        s, c = lax.div(sc, 3), lax.rem(sc, 3)
        return pltpu.make_async_remote_copy(
            src_ref=basis_ref.at[s, :, c, layers - 1], dst_ref=halo.at[sc],
            send_sem=halo_send.at[sc], recv_sem=halo_recv.at[sc],
            device_id=(w, group(1)), device_id_type=MESH)

    mat_copy = pltpu.make_async_copy(mat_ref, mats, small_sem.at[0])
    head_copy = pltpu.make_async_copy(slab_ref.at[pl.ds(0, 128)], head, small_sem.at[1])
    mat_halo_copy = pltpu.make_async_remote_copy(
        src_ref=mat_ref.at[:, layers - 1], dst_ref=mat_halo, send_sem=mat_send, recv_sem=mat_recv,
        device_id=(w, group(1)), device_id_type=MESH)

    mat_copy.start()
    for sc in range(6):
        load(sc).start()
    head_copy.start()

    barrier = pltpu.get_barrier_semaphore()

    def greet(d, carry):
        pl.semaphore_signal(barrier, inc=1, device_id=(w, group(d)), device_id_type=MESH)
        pl.semaphore_signal(barrier, inc=1, device_id=(across(d), n), device_id_type=MESH)
        return carry

    lax.fori_loop(1, count, greet, 0)
    pl.semaphore_wait(barrier, 2 * (count - 1))

    mat_halo_copy.start()
    for sc in range(6):
        halo_copy(sc).start()

    acc[...] = jnp.zeros_like(acc)
    late[...] = jnp.zeros_like(late)
    right[...] = jnp.zeros_like(right)
    pieces[...] = jnp.zeros_like(pieces)

    table = table_ref[...].astype(F32)
    mat_copy.wait()
    mat_halo_copy.wait()
    bottom = jnp.where(n == 0, 0.0, 1.0)
    top = jnp.where(n == count - 1, 1.0, 0.0)

    def lame(material):
        shear = jnp.zeros(material.shape, F32)
        dilate = jnp.zeros(material.shape, F32)
        for k in range(table.shape[1]):
            hit = material == k
            shear = jnp.where(hit, table[0:1, k:k + 1], shear)
            dilate = jnp.where(hit, table[1:2, k:k + 1], dilate)
        return shear, dilate

    for s in range(2):
        below = [x * bottom for x in lame(mat_halo[s])]
        cells = [lame(mats[s, i]) for i in range(layers)]
        for i in range(layers):
            here = cells[i]
            lower_x = below if i == 0 else cells[i - 1]

            def weights(other):
                m = 0.5 * (here[0] + other[0])
                return m, m + (m + 0.5 * (here[1] + other[1]))

            x_low = weights(lower_x)
            if i + 1 < layers:
                x_high = weights(cells[i + 1])
            else:
                x_high = [x * top for x in weights((jnp.zeros_like(here[0]),) * 2)]
            y_low = weights([shift_up(x, 0) for x in here])
            y_high = weights([shift_down(x, 0) for x in here])
            z_low = weights([shift_up(x, 1) for x in here])
            z_high = weights([shift_down(x, 1) for x in here])
            lane = lax.broadcasted_iota(jnp.int32, here[0].shape, 1)
            for c in range(3):
                px, py, pz = (int(c == d) for d in range(3))
                coef[3 * s + c, i, 0] = (x_low[px] + x_high[px]) + (y_low[py] + y_high[py]) + (z_low[pz] + z_high[pz])
                coef[3 * s + c, i, 1] = x_low[px]
                coef[3 * s + c, i, 2] = y_low[py]
                coef[3 * s + c, i, 3] = jnp.where(lane == 0, 0.0, z_low[pz])
                coef[3 * s + c, i, 4] = jnp.where(lane == lane.shape[1] - 1, 0.0, z_high[pz])
                if i == 0:
                    coef_halo[3 * s + c] = x_low[px] * bottom

    rows_y = 8

    def interior(sc, carry):
        s = lax.div(sc, 3)
        load(sc).wait()
        for i in range(layers):
            natural[i] = tiles[sc, :, i].astype(F32).reshape(funcs * rows_y, 128)

        def field(i, y):
            return natural[i, pl.ds(y, funcs, stride=rows_y), :]

        def k(i, which, y):
            return coef[sc, i, which, pl.ds(y, 1), :]

        for i in range(layers):
            for y in range(rows_y):
                v = field(i, y)
                image = k(i, 0, y) * v
                if i > 0:
                    image = image - k(i, 1, y) * field(i - 1, y)
                if i + 1 < layers:
                    image = image - k(i + 1, 1, y) * field(i + 1, y)
                if y > 0:
                    image = image - k(i, 2, y) * field(i, y - 1)
                if y + 1 < rows_y:
                    image = image - k(i, 2, y + 1) * field(i, y + 1)
                image = image - k(i, 3, y) * pltpu.roll(v, 1, 1) - k(i, 4, y) * pltpu.roll(v, 127, 1)
                lanes = slice(128 * y, 128 * (y + 1))
                hi, lo = split2(image)
                vb = v.astype(BF16)
                left[:, lanes] = vb
                if i == 0:
                    first[sc, :, lanes] = vb
                right[0:funcs, lanes] = hi
                right[128:128 + funcs, lanes] = lo
            acc[s] += lax.dot_general(left[...], right[...], NT, preferred_element_type=F32)
        return carry

    lax.fori_loop(0, 6, interior, 0)

    def boundary(sc, carry):
        s = lax.div(sc, 3)
        halo_copy(sc).wait()
        natural[0] = halo[sc].astype(F32).reshape(funcs * rows_y, 128)
        for y in range(rows_y):
            h = natural[0, pl.ds(y, funcs, stride=rows_y), :]
            hi, lo = split2(coef_halo[sc, pl.ds(y, 1), :] * h)
            lanes = slice(128 * y, 128 * (y + 1))
            left[:, lanes] = h.astype(BF16)
            right[0:funcs, lanes] = hi
            right[128:128 + funcs, lanes] = lo
        late[s, 0:funcs] += lax.dot_general(left[...], right[...], NT, preferred_element_type=F32)
        late[s, funcs:2 * funcs] += lax.dot_general(first[sc], right[...], NT, preferred_element_type=F32)
        return carry

    lax.fori_loop(0, 6, boundary, 0)

    head_copy.wait()
    mine = jnp.where(owner_ref[0] == n, 1.0, 0.0)
    for q in range(16):
        pieces[q, 16:24, :] = head[8 * q:8 * (q + 1), :].astype(F32) * mine
    for s in range(2):
        both = acc[s] + late[s, 0:funcs]
        total = both[:, 0:128] + both[:, 128:256]
        cross = late[s, funcs:2 * funcs, 0:128] + late[s, funcs:2 * funcs, 128:256]
        square = jnp.concatenate([cross, jnp.zeros((128 - funcs, 128), F32)], 0)
        total = total - cross - square.T[0:funcs]
        for z in range(8):
            pieces[2 * z + s, 0:12, :] = total[12 * z:12 * (z + 1), :]

    def rs_copy(d):
        return pltpu.make_async_remote_copy(
            src_ref=pieces.at[group(d)], dst_ref=landed.at[n], send_sem=rs_send.at[d], recv_sem=rs_recv.at[d],
            device_id=(w, group(d)), device_id_type=MESH)

    def wide_copy(d):
        return pltpu.make_async_remote_copy(
            src_ref=reduced, dst_ref=wide_in.at[w], send_sem=wide_send.at[d], recv_sem=wide_recv.at[d],
            device_id=(across(d), n), device_id_type=MESH)

    def own_copy(d):
        return pltpu.make_async_remote_copy(
            src_ref=reduced, dst_ref=own_ref.at[n], send_sem=own_send.at[d], recv_sem=own_recv.at[d],
            device_id=(w, group(d)), device_id_type=MESH)

    def panel_copy(d):
        return pltpu.make_async_remote_copy(
            src_ref=chosen, dst_ref=panel_ref.at[n], send_sem=panel_send.at[d], recv_sem=panel_recv.at[d],
            device_id=(w, group(d)), device_id_type=MESH)

    def start_all(copy):
        lax.fori_loop(1, count, lambda d, carry: (copy(d).start(), carry)[1], 0)

    def wait_all(copy):
        lax.fori_loop(1, count, lambda d, carry: (copy(d).wait(), carry)[1], 0)

    start_all(rs_copy)
    landed[n] = pieces[n]
    wait_all(rs_copy)
    total = landed[0]
    for q in range(1, 16):
        total = total + landed[q]
    reduced[...] = total
    reduced[12:14, :] = jnp.full((2, 128), -1.0, F32)
    reduced[12:14, 0:funcs] = ids_ref[...].astype(F32)
    start_all(wide_copy)
    start_all(own_copy)
    own_ref[n] = reduced[...]
    wide_in[w] = reduced[...]
    wait_all(wide_copy)
    chosen[...] = wide_in[owner_ref[0]]
    start_all(panel_copy)
    panel_ref[n] = chosen[...]
    wait_all(own_copy)
    wait_all(panel_copy)


def gather(owner, table, ids, basis, mat, slab):
    subs, funcs, comps, layers, rows_y, depth = basis.shape
    vmem, anyspace = pl.BlockSpec(memory_space=pltpu.VMEM), pl.BlockSpec(memory_space=pl.ANY)
    dma = pltpu.SemaphoreType.DMA
    piece = jax.ShapeDtypeStruct((16, PIECE, 128), F32)
    return pl.pallas_call(
        gather_kernel,
        out_shape=(piece, piece),
        in_specs=[pl.BlockSpec(memory_space=pltpu.SMEM), vmem, vmem, anyspace, anyspace, anyspace],
        out_specs=(vmem, vmem),
        scratch_shapes=[
            pltpu.VMEM((6, funcs, layers, rows_y, depth), BF16),
            pltpu.VMEM((6, funcs, rows_y, depth), BF16),
            pltpu.VMEM((subs, layers, rows_y, depth), jnp.int32),
            pltpu.VMEM((subs, rows_y, depth), jnp.int32),
            pltpu.VMEM((128, 128), BF16),
            pltpu.VMEM((6, layers, 5, rows_y, depth), F32),
            pltpu.VMEM((6, rows_y, depth), F32),
            pltpu.VMEM((layers, funcs * rows_y, depth), F32),
            pltpu.VMEM((funcs, rows_y * depth), BF16),
            pltpu.VMEM((256, rows_y * depth), BF16),
            pltpu.VMEM((6, funcs, rows_y * depth), BF16),
            pltpu.VMEM((subs, funcs, 256), F32),
            pltpu.VMEM((subs, 2 * funcs, 256), F32),
            pltpu.VMEM((16, PIECE, 128), F32),
            pltpu.VMEM((16, PIECE, 128), F32),
            pltpu.VMEM((PIECE, 128), F32),
            pltpu.VMEM((16, PIECE, 128), F32),
            pltpu.VMEM((PIECE, 128), F32),
            dma((6,)), dma((2,)), dma((6,)), dma((6,)), dma, dma,
            dma((16,)), dma((16,)), dma((16,)), dma((16,)), dma((16,)), dma((16,)), dma((16,)), dma((16,)),
        ],
        compiler_params=pltpu.CompilerParams(collective_id=0, has_side_effects=True, vmem_limit_bytes=56 << 20),
        name="galerkin_gather",
    )(owner, table, ids, basis, mat, slab)


def panel_kernel(owner_ref, panel_ref, own_ref, column_ref, rows_ref, slab_ref, out_ref, galerkin_ref, block, added_own, lower, parts, rows_bf):
    w, n = lax.axis_index("wide"), lax.axis_index("narrow")
    owner = owner_ref[0]
    funcs = galerkin_ref.shape[1]
    height, tile = out_ref.shape[0], 512

    def slots(pieces_ref, s):
        ids = pieces_ref[0, 12 + s:13 + s, :]
        index = lax.broadcasted_iota(jnp.int32, (128, 128), 0).astype(F32)
        return jnp.where(index == ids, 1.0, 0.0)

    def added_of(pieces_ref):
        total = jnp.zeros((128, 128), F32)
        for s in range(2):
            place = slots(pieces_ref, s)
            for z in range(8):
                block[12 * z:12 * (z + 1), :] = pieces_ref[2 * z + s, 0:12, :]
            total = total + exact_dot(exact_dot(place, block[...], NN), place, NT)
        return total

    block[...] = jnp.zeros_like(block)
    for s in range(2):
        for z in range(8):
            galerkin_ref[s, 12 * z:12 * (z + 1), :] = own_ref[2 * z + s, 0:12, 0:funcs]

    diagonal = added_of(panel_ref) + jnp.concatenate([panel_ref[q, 16:24, :] for q in range(16)], 0)
    diagonal = 0.5 * (diagonal + diagonal.T)
    sub = lax.broadcasted_iota(jnp.int32, (8, 128), 0)
    lane = lax.broadcasted_iota(jnp.int32, (8, 128), 1)
    a = [diagonal[8 * b:8 * (b + 1)] for b in range(16)]
    m = [jnp.where(lane == sub + 8 * b, 1.0, 0.0) for b in range(16)]
    for j in range(128):
        b0, r = divmod(j, 8)
        row_a, row_m = a[b0][r:r + 1], m[b0][r:r + 1]
        inverse = 1.0 / row_a[:, j:j + 1]
        row_a, row_m = row_a * inverse, row_m * inverse
        for b in range(b0, 16):
            if b == b0 and r == 7:
                continue
            f = a[b][:, j:j + 1]
            if b == b0:
                f = jnp.where(sub[:, 0:1] > r, f, 0.0)
            a[b] = a[b] - f * row_a
            m[b] = m[b] - f * row_m
    upper = []
    for b in range(16):
        on_diagonal = lane == sub + 8 * b
        d = jnp.sum(jnp.where(on_diagonal, a[b], 0.0), axis=1, keepdims=True)
        scale = lax.rsqrt(d)
        upper.append(jnp.where(lane >= sub + 8 * b, a[b] * scale, 0.0))
        m[b] = m[b] * scale
    lower[...] = jnp.concatenate(upper, 0).T
    inverse = jnp.concatenate(m, 0)
    hi, rest = split2(inverse)
    mid, low = split2(inverse - hi.astype(F32))
    parts[0:128] = hi
    parts[128:256] = mid
    parts[256:384] = low

    def solve(x):
        y = lax.dot_general(x, parts[...], NT, preferred_element_type=F32)
        return y[:, 0:128] + (y[:, 128:256] + y[:, 256:384])

    rows_bf[...] = solve(rows_ref[...]).astype(BF16)
    added_own[...] = jnp.zeros_like(added_own)

    @pl.when((w == n) & (n >= owner))
    def _():
        added_own[...] = added_of(own_ref)

    def store(start, size, factor, base):
        part = pl.ds(start, size)

        @pl.when(n > owner)
        def _():
            update = lax.dot_general(factor, rows_bf[...], NT, preferred_element_type=F32)
            out_ref[part, :] = (base - update).astype(BF16)

        @pl.when(n == owner)
        def _():
            out_ref[part, :] = factor

        @pl.when(n < owner)
        def _():
            out_ref[part, :] = base.astype(BF16)

    solved = solve(column_ref[0:128, :])
    solved = jnp.where(w == owner, lower[...], solved)
    solved = jnp.where(w < owner, 0.0, solved)
    store(0, 128, solved.astype(BF16), slab_ref[0:128, :].astype(F32) + added_own[...])

    def body(t, carry):
        start = pl.multiple_of(128 + t * tile, 128)
        part = pl.ds(start, tile)
        store(start, tile, solve(column_ref[part, :]).astype(BF16), slab_ref[part, :].astype(F32))
        return carry

    steps = (height - 128) // tile
    lax.fori_loop(0, steps, body, 0)
    done = 128 + steps * tile
    rest = slice(done, height)
    store(done, height - done, solve(column_ref[rest, :]).astype(BF16), slab_ref[rest, :].astype(F32))


def panel_step(owner, panel, own, column, rows, slab, funcs):
    vmem = pl.BlockSpec(memory_space=pltpu.VMEM)
    return pl.pallas_call(
        panel_kernel,
        out_shape=(jax.ShapeDtypeStruct(slab.shape, BF16), jax.ShapeDtypeStruct((2, funcs, funcs), F32)),
        in_specs=[pl.BlockSpec(memory_space=pltpu.SMEM)] + [vmem] * 5,
        out_specs=(vmem, vmem),
        scratch_shapes=[
            pltpu.VMEM((128, 128), F32), pltpu.VMEM((128, 128), F32), pltpu.VMEM((128, 128), F32),
            pltpu.VMEM((384, 128), BF16), pltpu.VMEM((128, 128), BF16),
        ],
        compiler_params=pltpu.CompilerParams(vmem_limit_bytes=48 << 20),
        name="panel_step",
    )(owner, panel, own, column, rows, slab)


def on_device(coarse_basis, material_ids, lame_table, coarse_ids, coarse_slab, panel_owner):
    w, n = lax.axis_index("wide"), lax.axis_index("narrow")
    column = lax.psum(jnp.where(n == panel_owner[0], coarse_slab, 0).astype(BF16), "narrow")
    rows = lax.psum(jnp.where(w == n, column[:128], 0).astype(BF16), "wide")
    own, panel = gather(panel_owner, lame_table, coarse_ids, coarse_basis, material_ids, coarse_slab)
    return panel_step(panel_owner, panel, own, column, rows, coarse_slab, coarse_basis.shape[1])


def solution(mesh):
    return jax.shard_map(
        on_device,
        mesh=mesh,
        in_specs=(
            P("wide", None, None, "narrow", None, None),
            P("wide", "narrow", None, None),
            P(),
            P("wide", None),
            P("wide", "narrow"),
            P(),
        ),
        out_specs=(P("wide", "narrow"), P("wide", None, None)),
        check_vma=False,
    )
```

```python
import functools

import jax
import jax.numpy as jnp
from jax import lax
from jax.experimental import pallas as pl
from jax.experimental.pallas import tpu as pltpu
from jax.sharding import PartitionSpec as P

MESH = pl.DeviceIdType.MESH
F32, BF16 = jnp.float32, jnp.bfloat16
NT = (((1,), (1,)), ((), ()))
NN = (((1,), (0,)), ((), ()))
PIECE = 24
WIDER = 32
STREAMS = 4
RING = 8


def exact_dot(a, b, dims):
    return lax.dot_general(a, b, dims, precision=lax.Precision.HIGHEST, preferred_element_type=F32)


def split2(x):
    hi = x.astype(BF16)
    return hi, (x - hi.astype(F32)).astype(BF16)


def shift_up(x, axis):
    index = lax.broadcasted_iota(jnp.int32, x.shape, axis)
    return jnp.where(index == 0, 0.0, pltpu.roll(x, 1, axis))


def shift_down(x, axis):
    size = x.shape[axis]
    index = lax.broadcasted_iota(jnp.int32, x.shape, axis)
    return jnp.where(index == size - 1, 0.0, pltpu.roll(x, size - 1, axis))


def gather_kernel(
    owner_ref, table_ref, ids_ref, basis_ref, mat_ref, slab_ref,
    own_ref, panel_ref, column_ref,
    tiles, halo, mats, mat_halo, coef, coef_halo, natural, left, right, first, acc, late,
    pieces, landed, reduced, wide_in, chosen, slab, passing, swapped,
    load_sem, small_sem, halo_send, halo_recv, mat_send, mat_recv, rs_send, rs_recv,
    wide_send, wide_recv, own_send, own_recv, panel_send, panel_recv,
    ring_send, ring_recv, swap_send, swap_recv, spread_send, spread_recv,
):
    w, n = lax.axis_index("wide"), lax.axis_index("narrow")
    count = lax.axis_size("narrow")
    funcs = basis_ref.shape[1]
    layers = basis_ref.shape[3]
    group = lambda d: lax.rem(n + d, count)
    across = lambda d: lax.rem(w + d, count)

    def load(sc):
        s, c = lax.div(sc, 3), lax.rem(sc, 3)
        return pltpu.make_async_copy(basis_ref.at[s, :, c], tiles.at[sc], load_sem.at[sc])

    def halo_copy(sc):
        s, c = lax.div(sc, 3), lax.rem(sc, 3)
        return pltpu.make_async_remote_copy(
            src_ref=basis_ref.at[s, :, c, layers - 1], dst_ref=halo.at[sc],
            send_sem=halo_send.at[sc], recv_sem=halo_recv.at[sc],
            device_id=(w, group(1)), device_id_type=MESH)

    z, half = lax.div(n, 2), lax.rem(n, 2)
    piece_rows = column_ref.shape[0] // RING
    chunk = piece_rows // STREAMS
    way = lambda t: 1 if t % 2 == 0 else RING - 1
    beside = lambda t: 2 * lax.rem(z + way(t), RING) + half
    piece_at = lambda t, k: lax.rem(z + (RING - way(t)) * k, RING)

    def chunk_rows(t, piece):
        return pl.ds(pl.multiple_of(piece * piece_rows + t * chunk, chunk), chunk)

    def ring_copy(t, k, source=None):
        return pltpu.make_async_remote_copy(
            src_ref=passing.at[t, k - 1] if source is None else source, dst_ref=passing.at[t, k],
            send_sem=ring_send.at[t, k], recv_sem=ring_recv.at[t, k],
            device_id=(w, beside(t)), device_id_type=MESH)

    def ring_start(t):
        ring_copy(t, 0, slab.at[chunk_rows(t, piece_at(t, 1))]).start()

    def ring_land(t, k):
        ring_copy(t, k, passing.at[t, k]).wait()
        passing[t, k] += slab[chunk_rows(t, piece_at(t, k + 2)), :]

    def swap_copy(t):
        return pltpu.make_async_remote_copy(
            src_ref=passing.at[t, RING - 2], dst_ref=swapped.at[t], send_sem=swap_send.at[t], recv_sem=swap_recv.at[t],
            device_id=(w, n + 1 - 2 * half), device_id_type=MESH)

    def spread_copy(t, k):
        part = column_ref.at[chunk_rows(t, piece_at(t, k))]
        return pltpu.make_async_remote_copy(
            src_ref=part, dst_ref=part, send_sem=spread_send.at[t, k], recv_sem=spread_recv.at[t, k],
            device_id=(w, beside(t)), device_id_type=MESH)

    def spread_step(k):
        for t in range(STREAMS):
            spread_copy(t, k).wait()
            if k + 1 < RING - 1:
                spread_copy(t, k + 1).start()

    mat_copy = pltpu.make_async_copy(mat_ref, mats, small_sem.at[0])
    slab_copy = pltpu.make_async_copy(slab_ref, slab, small_sem.at[1])
    mat_halo_copy = pltpu.make_async_remote_copy(
        src_ref=mat_ref.at[:, layers - 1], dst_ref=mat_halo, send_sem=mat_send, recv_sem=mat_recv,
        device_id=(w, group(1)), device_id_type=MESH)

    slab_copy.start()
    mat_copy.start()
    for sc in range(6):
        load(sc).start()

    barrier = pltpu.get_barrier_semaphore()

    def greet(d, carry):
        pl.semaphore_signal(barrier, inc=1, device_id=(w, group(d)), device_id_type=MESH)
        pl.semaphore_signal(barrier, inc=1, device_id=(across(d), n), device_id_type=MESH)
        return carry

    lax.fori_loop(1, count, greet, 0)
    mine = jnp.where(owner_ref[0] == n, 1.0, 0.0).astype(BF16)
    slab_copy.wait()

    def mask(q, carry):
        part = pl.ds(pl.multiple_of(q * piece_rows, piece_rows), piece_rows)
        slab[part, :] = slab[part, :] * mine
        return carry

    lax.fori_loop(0, RING, mask, 0)
    pl.semaphore_wait(barrier, 2 * (count - 1))

    mat_halo_copy.start()
    for sc in range(6):
        halo_copy(sc).start()
    for t in range(STREAMS):
        ring_start(t)

    acc[...] = jnp.zeros_like(acc)
    late[...] = jnp.zeros_like(late)
    right[...] = jnp.zeros_like(right)
    pieces[...] = jnp.zeros_like(pieces)

    table = table_ref[...].astype(F32)
    mat_copy.wait()
    mat_halo_copy.wait()
    bottom = jnp.where(n == 0, 0.0, 1.0)
    top = jnp.where(n == count - 1, 1.0, 0.0)

    def lame(material):
        shear = jnp.zeros(material.shape, F32)
        dilate = jnp.zeros(material.shape, F32)
        for k in range(table.shape[1]):
            hit = material == k
            shear = jnp.where(hit, table[0:1, k:k + 1], shear)
            dilate = jnp.where(hit, table[1:2, k:k + 1], dilate)
        return shear, dilate

    for s in range(2):
        below = [x * bottom for x in lame(mat_halo[s])]
        cells = [lame(mats[s, i]) for i in range(layers)]
        for i in range(layers):
            here = cells[i]
            lower_x = below if i == 0 else cells[i - 1]

            def weights(other):
                m = 0.5 * (here[0] + other[0])
                return m, m + (m + 0.5 * (here[1] + other[1]))

            x_low = weights(lower_x)
            if i + 1 < layers:
                x_high = weights(cells[i + 1])
            else:
                x_high = [x * top for x in weights((jnp.zeros_like(here[0]),) * 2)]
            y_low = weights([shift_up(x, 0) for x in here])
            y_high = weights([shift_down(x, 0) for x in here])
            z_low = weights([shift_up(x, 1) for x in here])
            z_high = weights([shift_down(x, 1) for x in here])
            lane = lax.broadcasted_iota(jnp.int32, here[0].shape, 1)
            for c in range(3):
                px, py, pz = (int(c == d) for d in range(3))
                coef[3 * s + c, i, 0] = (x_low[px] + x_high[px]) + (y_low[py] + y_high[py]) + (z_low[pz] + z_high[pz])
                coef[3 * s + c, i, 1] = x_low[px]
                coef[3 * s + c, i, 2] = y_low[py]
                coef[3 * s + c, i, 3] = jnp.where(lane == 0, 0.0, z_low[pz])
                coef[3 * s + c, i, 4] = jnp.where(lane == lane.shape[1] - 1, 0.0, z_high[pz])
                if i == 0:
                    coef_halo[3 * s + c] = x_low[px] * bottom

    rows_y = 8

    def interior(sc, carry):
        s = lax.div(sc, 3)
        load(sc).wait()
        for i in range(layers):
            natural[i] = tiles[sc, :, i].astype(F32).reshape(funcs * rows_y, 128)

        def field(i, y):
            return natural[i, pl.ds(y, funcs, stride=rows_y), :]

        def k(i, which, y):
            return coef[sc, i, which, pl.ds(y, 1), :]

        for i in range(layers):
            for y in range(rows_y):
                v = field(i, y)
                image = k(i, 0, y) * v
                if i > 0:
                    image = image - k(i, 1, y) * field(i - 1, y)
                if i + 1 < layers:
                    image = image - k(i + 1, 1, y) * field(i + 1, y)
                if y > 0:
                    image = image - k(i, 2, y) * field(i, y - 1)
                if y + 1 < rows_y:
                    image = image - k(i, 2, y + 1) * field(i, y + 1)
                image = image - k(i, 3, y) * pltpu.roll(v, 1, 1) - k(i, 4, y) * pltpu.roll(v, 127, 1)
                lanes = slice(128 * y, 128 * (y + 1))
                hi, lo = split2(image)
                vb = v.astype(BF16)
                left[:, lanes] = vb
                if i == 0:
                    first[sc, :, lanes] = vb
                right[0:funcs, lanes] = hi
                right[128:128 + funcs, lanes] = lo
            acc[s] += lax.dot_general(left[...], right[...], NT, preferred_element_type=F32)
            ring_land(i, sc)
            ring_copy(i, sc + 1).start()
        return carry

    lax.fori_loop(0, 6, interior, 0)
    for t in range(STREAMS):
        ring_land(t, RING - 2)
        swap_copy(t).start()
    for t in range(STREAMS):
        swap_copy(t).wait()
        column_ref[chunk_rows(t, z), :] = passing[t, RING - 2] + swapped[t]
        spread_copy(t, 0).start()

    def boundary(sc, carry):
        s = lax.div(sc, 3)
        halo_copy(sc).wait()
        natural[0] = halo[sc].astype(F32).reshape(funcs * rows_y, 128)
        for y in range(rows_y):
            h = natural[0, pl.ds(y, funcs, stride=rows_y), :]
            hi, lo = split2(coef_halo[sc, pl.ds(y, 1), :] * h)
            lanes = slice(128 * y, 128 * (y + 1))
            left[:, lanes] = h.astype(BF16)
            right[0:funcs, lanes] = hi
            right[128:128 + funcs, lanes] = lo
        late[s, 0:funcs] += lax.dot_general(left[...], right[...], NT, preferred_element_type=F32)
        late[s, funcs:2 * funcs] += lax.dot_general(first[sc], right[...], NT, preferred_element_type=F32)
        return carry

    lax.fori_loop(0, 3, boundary, 0)
    spread_step(0)
    lax.fori_loop(3, 6, boundary, 0)

    head = slab[0:128, :].astype(F32)
    for q in range(16):
        pieces[q, 16:24, :] = head[8 * q:8 * (q + 1), :]
    for s in range(2):
        both = acc[s] + late[s, 0:funcs]
        total = both[:, 0:128] + both[:, 128:256]
        cross = late[s, funcs:2 * funcs, 0:128] + late[s, funcs:2 * funcs, 128:256]
        square = jnp.concatenate([cross, jnp.zeros((128 - funcs, 128), F32)], 0)
        total = total - cross - square.T[0:funcs]
        for part in range(RING):
            pieces[2 * part + s, 0:12, :] = total[12 * part:12 * (part + 1), :]

    def rs_copy(d):
        return pltpu.make_async_remote_copy(
            src_ref=pieces.at[group(d)], dst_ref=landed.at[n], send_sem=rs_send.at[d], recv_sem=rs_recv.at[d],
            device_id=(w, group(d)), device_id_type=MESH)

    def wide_copy(d):
        return pltpu.make_async_remote_copy(
            src_ref=reduced, dst_ref=wide_in.at[w], send_sem=wide_send.at[d], recv_sem=wide_recv.at[d],
            device_id=(across(d), n), device_id_type=MESH)

    def own_copy(d):
        return pltpu.make_async_remote_copy(
            src_ref=reduced, dst_ref=own_ref.at[n], send_sem=own_send.at[d], recv_sem=own_recv.at[d],
            device_id=(w, group(d)), device_id_type=MESH)

    def panel_copy(d):
        return pltpu.make_async_remote_copy(
            src_ref=chosen.at[group(d)], dst_ref=panel_ref.at[n], send_sem=panel_send.at[d], recv_sem=panel_recv.at[d],
            device_id=(w, group(d)), device_id_type=MESH)

    def start_all(copy):
        lax.fori_loop(1, count, lambda d, carry: (copy(d).start(), carry)[1], 0)

    def wait_all(copy):
        lax.fori_loop(1, count, lambda d, carry: (copy(d).wait(), carry)[1], 0)

    start_all(rs_copy)
    landed[n] = pieces[n]
    spread_step(1)
    spread_step(2)
    wait_all(rs_copy)
    total = landed[0]
    for q in range(1, 16):
        total = total + landed[q]
    reduced[...] = total
    reduced[12:14, :] = jnp.full((2, 128), -1.0, F32)
    reduced[12:14, 0:funcs] = ids_ref[...].astype(F32)
    start_all(wide_copy)
    start_all(own_copy)
    own_ref[n] = reduced[...]
    wide_in[w] = reduced[...]
    spread_step(3)
    wait_all(wide_copy)
    of_owner = wide_in[owner_ref[0]]
    for q in range(16):
        chosen[q, 0:24, :] = of_owner
        chosen[q, 24:32, :] = wide_in[q, 16:24, :]
    start_all(panel_copy)
    panel_ref[n] = chosen[n]
    for k in range(4, RING - 1):
        spread_step(k)
    wait_all(own_copy)
    wait_all(panel_copy)


def gather(owner, table, ids, basis, mat, slab):
    subs, funcs, comps, layers, rows_y, depth = basis.shape
    vmem, anyspace = pl.BlockSpec(memory_space=pltpu.VMEM), pl.BlockSpec(memory_space=pl.ANY)
    dma = pltpu.SemaphoreType.DMA
    piece = jax.ShapeDtypeStruct((16, PIECE, 128), F32)
    wider = jax.ShapeDtypeStruct((16, WIDER, 128), F32)
    chunk = slab.shape[0] // RING // STREAMS
    return pl.pallas_call(
        gather_kernel,
        out_shape=(piece, wider, jax.ShapeDtypeStruct(slab.shape, BF16)),
        in_specs=[pl.BlockSpec(memory_space=pltpu.SMEM), vmem, vmem, anyspace, anyspace, anyspace],
        out_specs=(vmem, vmem, vmem),
        scratch_shapes=[
            pltpu.VMEM((6, funcs, layers, rows_y, depth), BF16),
            pltpu.VMEM((6, funcs, rows_y, depth), BF16),
            pltpu.VMEM((subs, layers, rows_y, depth), jnp.int32),
            pltpu.VMEM((subs, rows_y, depth), jnp.int32),
            pltpu.VMEM((6, layers, 5, rows_y, depth), F32),
            pltpu.VMEM((6, rows_y, depth), F32),
            pltpu.VMEM((layers, funcs * rows_y, depth), F32),
            pltpu.VMEM((funcs, rows_y * depth), BF16),
            pltpu.VMEM((256, rows_y * depth), BF16),
            pltpu.VMEM((6, funcs, rows_y * depth), BF16),
            pltpu.VMEM((subs, funcs, 256), F32),
            pltpu.VMEM((subs, 2 * funcs, 256), F32),
            pltpu.VMEM((16, PIECE, 128), F32),
            pltpu.VMEM((16, PIECE, 128), F32),
            pltpu.VMEM((PIECE, 128), F32),
            pltpu.VMEM((16, PIECE, 128), F32),
            pltpu.VMEM((16, WIDER, 128), F32),
            pltpu.VMEM(slab.shape, BF16),
            pltpu.VMEM((STREAMS, RING - 1, chunk, 128), BF16),
            pltpu.VMEM((STREAMS, chunk, 128), BF16),
            dma((6,)), dma((2,)), dma((6,)), dma((6,)), dma, dma,
            dma((16,)), dma((16,)), dma((16,)), dma((16,)), dma((16,)), dma((16,)), dma((16,)), dma((16,)),
            dma((STREAMS, RING - 1)), dma((STREAMS, RING - 1)), dma((STREAMS,)), dma((STREAMS,)),
            dma((STREAMS, RING - 1)), dma((STREAMS, RING - 1)),
        ],
        compiler_params=pltpu.CompilerParams(collective_id=0, has_side_effects=True, vmem_limit_bytes=56 << 20),
        name="galerkin_gather",
    )(owner, table, ids, basis, mat, slab)


def panel_kernel(owner_ref, panel_ref, own_ref, column_ref, slab_ref, out_ref, galerkin_ref, block, added_own, lower, parts, rows_bf):
    w, n = lax.axis_index("wide"), lax.axis_index("narrow")
    owner = owner_ref[0]
    funcs = galerkin_ref.shape[1]
    height, tile = out_ref.shape[0], 512

    def slots(pieces_ref, s):
        ids = pieces_ref[0, 12 + s:13 + s, :]
        index = lax.broadcasted_iota(jnp.int32, (128, 128), 0).astype(F32)
        return jnp.where(index == ids, 1.0, 0.0)

    def added_of(pieces_ref):
        total = jnp.zeros((128, 128), F32)
        for s in range(2):
            place = slots(pieces_ref, s)
            for z in range(8):
                block[12 * z:12 * (z + 1), :] = pieces_ref[2 * z + s, 0:12, :]
            total = total + exact_dot(exact_dot(place, block[...], NN), place, NT)
        return total

    block[...] = jnp.zeros_like(block)
    for s in range(2):
        for z in range(8):
            galerkin_ref[s, 12 * z:12 * (z + 1), :] = own_ref[2 * z + s, 0:12, 0:funcs]

    diagonal = added_of(panel_ref) + jnp.concatenate([panel_ref[q, 16:24, :] for q in range(16)], 0)
    diagonal = 0.5 * (diagonal + diagonal.T)
    sub = lax.broadcasted_iota(jnp.int32, (8, 128), 0)
    lane = lax.broadcasted_iota(jnp.int32, (8, 128), 1)
    a = [diagonal[8 * b:8 * (b + 1)] for b in range(16)]
    m = [jnp.where(lane == sub + 8 * b, 1.0, 0.0) for b in range(16)]
    for j in range(128):
        b0, r = divmod(j, 8)
        row_a, row_m = a[b0][r:r + 1], m[b0][r:r + 1]
        inverse = 1.0 / row_a[:, j:j + 1]
        row_a, row_m = row_a * inverse, row_m * inverse
        for b in range(b0, 16):
            if b == b0 and r == 7:
                continue
            f = a[b][:, j:j + 1]
            if b == b0:
                f = jnp.where(sub[:, 0:1] > r, f, 0.0)
            a[b] = a[b] - f * row_a
            m[b] = m[b] - f * row_m
    upper = []
    for b in range(16):
        on_diagonal = lane == sub + 8 * b
        d = jnp.sum(jnp.where(on_diagonal, a[b], 0.0), axis=1, keepdims=True)
        scale = lax.rsqrt(d)
        upper.append(jnp.where(lane >= sub + 8 * b, a[b] * scale, 0.0))
        m[b] = m[b] * scale
    lower[...] = jnp.concatenate(upper, 0).T
    inverse = jnp.concatenate(m, 0)
    hi, rest = split2(inverse)
    mid, low = split2(inverse - hi.astype(F32))
    parts[0:128] = hi
    parts[128:256] = mid
    parts[256:384] = low

    def solve(x):
        y = lax.dot_general(x, parts[...], NT, preferred_element_type=F32)
        return y[:, 0:128] + (y[:, 128:256] + y[:, 256:384])

    rows = jnp.concatenate([panel_ref[q, 24:32, :] for q in range(16)], 0)
    rows_bf[...] = solve(rows.astype(BF16)).astype(BF16)
    added_own[...] = jnp.zeros_like(added_own)

    @pl.when((w == n) & (n >= owner))
    def _():
        added_own[...] = added_of(own_ref)

    def store(start, size, factor, base):
        part = pl.ds(start, size)

        @pl.when(n > owner)
        def _():
            update = lax.dot_general(factor, rows_bf[...], NT, preferred_element_type=F32)
            out_ref[part, :] = (base - update).astype(BF16)

        @pl.when(n == owner)
        def _():
            out_ref[part, :] = factor

        @pl.when(n < owner)
        def _():
            out_ref[part, :] = base.astype(BF16)

    solved = solve(column_ref[0:128, :])
    solved = jnp.where(w == owner, lower[...], solved)
    solved = jnp.where(w < owner, 0.0, solved)
    store(0, 128, solved.astype(BF16), slab_ref[0:128, :].astype(F32) + added_own[...])

    def body(t, carry):
        start = pl.multiple_of(128 + t * tile, 128)
        part = pl.ds(start, tile)
        store(start, tile, solve(column_ref[part, :]).astype(BF16), slab_ref[part, :].astype(F32))
        return carry

    steps = (height - 128) // tile
    lax.fori_loop(0, steps, body, 0)
    done = 128 + steps * tile
    rest = slice(done, height)
    store(done, height - done, solve(column_ref[rest, :]).astype(BF16), slab_ref[rest, :].astype(F32))


def panel_step(owner, panel, own, column, slab, funcs):
    vmem = pl.BlockSpec(memory_space=pltpu.VMEM)
    return pl.pallas_call(
        panel_kernel,
        out_shape=(jax.ShapeDtypeStruct(slab.shape, BF16), jax.ShapeDtypeStruct((2, funcs, funcs), F32)),
        in_specs=[pl.BlockSpec(memory_space=pltpu.SMEM)] + [vmem] * 4,
        out_specs=(vmem, vmem),
        scratch_shapes=[
            pltpu.VMEM((128, 128), F32), pltpu.VMEM((128, 128), F32), pltpu.VMEM((128, 128), F32),
            pltpu.VMEM((384, 128), BF16), pltpu.VMEM((128, 128), BF16),
        ],
        compiler_params=pltpu.CompilerParams(vmem_limit_bytes=48 << 20),
        name="panel_step",
    )(owner, panel, own, column, slab)


def on_device(coarse_basis, material_ids, lame_table, coarse_ids, coarse_slab, panel_owner):
    own, panel, column = gather(panel_owner, lame_table, coarse_ids, coarse_basis, material_ids, coarse_slab)
    return panel_step(panel_owner, panel, own, column, coarse_slab, coarse_basis.shape[1])


def solution(mesh):
    return jax.shard_map(
        on_device,
        mesh=mesh,
        in_specs=(
            P("wide", None, None, "narrow", None, None),
            P("wide", "narrow", None, None),
            P(),
            P("wide", None),
            P("wide", "narrow"),
            P(),
        ),
        out_specs=(P("wide", "narrow"), P("wide", None, None)),
        check_vma=False,
    )
```

```python
import functools

import jax
import jax.numpy as jnp
from jax import lax
from jax.experimental import pallas as pl
from jax.experimental.pallas import tpu as pltpu
from jax.sharding import PartitionSpec as P

MESH = pl.DeviceIdType.MESH
F32, BF16 = jnp.float32, jnp.bfloat16
NT = (((1,), (1,)), ((), ()))
NN = (((1,), (0,)), ((), ()))
PIECE = 24
WIDER = 32
RING = 8
CHUNKS = 2
STREAMS = ((-1, 4, 0), (-1, 4, 1), (1, 3, 0), (1, 3, 1))


def exact_dot(a, b, dims):
    return lax.dot_general(a, b, dims, precision=lax.Precision.HIGHEST, preferred_element_type=F32)


def split2(x):
    hi = x.astype(BF16)
    return hi, (x - hi.astype(F32)).astype(BF16)


def shift_up(x, axis):
    index = lax.broadcasted_iota(jnp.int32, x.shape, axis)
    return jnp.where(index == 0, 0.0, pltpu.roll(x, 1, axis))


def shift_down(x, axis):
    size = x.shape[axis]
    index = lax.broadcasted_iota(jnp.int32, x.shape, axis)
    return jnp.where(index == size - 1, 0.0, pltpu.roll(x, size - 1, axis))


def gather_kernel(
    owner_ref, table_ref, ids_ref, basis_ref, mat_ref, slab_ref,
    own_ref, panel_ref, column_ref,
    tiles, halo, mats, mat_halo, coef, coef_halo, natural, left, right, first, acc, late,
    pieces, landed, reduced, wide_in, chosen, masked, passing, settled, swapped,
    load_sem, small_sem, halo_send, halo_recv, mat_send, mat_recv, rs_send, rs_recv,
    wide_send, wide_recv, own_send, own_recv, panel_send, panel_recv,
    ring_send, ring_recv, swap_send, swap_recv, spread_send, spread_recv,
):
    w, n = lax.axis_index("wide"), lax.axis_index("narrow")
    count = lax.axis_size("narrow")
    funcs = basis_ref.shape[1]
    layers = basis_ref.shape[3]
    group = lambda d: lax.rem(n + d, count)
    across = lambda d: lax.rem(w + d, count)

    def load(sc):
        s, c = lax.div(sc, 3), lax.rem(sc, 3)
        return pltpu.make_async_copy(basis_ref.at[s, :, c], tiles.at[sc], load_sem.at[sc])

    def halo_copy(sc):
        s, c = lax.div(sc, 3), lax.rem(sc, 3)
        return pltpu.make_async_remote_copy(
            src_ref=basis_ref.at[s, :, c, layers - 1], dst_ref=halo.at[sc],
            send_sem=halo_send.at[sc], recv_sem=halo_recv.at[sc],
            device_id=(w, group(1)), device_id_type=MESH)

    z, half = lax.div(n, 2), lax.rem(n, 2)
    piece_rows = column_ref.shape[0] // RING
    chunk = piece_rows // CHUNKS
    ring = lambda shift: lax.rem(z + shift + RING, RING)
    beside = lambda t: 2 * ring(STREAMS[t][0]) + half

    def chunk_rows(c, piece):
        return pl.ds(pl.multiple_of(piece * piece_rows + c * chunk, chunk), chunk)

    def ring_copy(t, k, source=None):
        return pltpu.make_async_remote_copy(
            src_ref=passing.at[t, k - 1] if source is None else source, dst_ref=passing.at[t, k],
            send_sem=ring_send.at[t, k], recv_sem=ring_recv.at[t, k],
            device_id=(w, beside(t)), device_id_type=MESH)

    def ring_start(t):
        way, steps, c = STREAMS[t]
        ring_copy(t, 0, masked.at[chunk_rows(c, ring(way * steps))]).start()

    def ring_step(t, k, last):
        way, steps, c = STREAMS[t]
        ring_copy(t, k, passing.at[t, k]).wait()
        if not last:
            passing[t, k] += masked[chunk_rows(c, ring(way * (steps - 1 - k))), :]
            ring_copy(t, k + 1, passing.at[t, k]).start()

    def swap_copy(c):
        return pltpu.make_async_remote_copy(
            src_ref=settled.at[c], dst_ref=swapped.at[c], send_sem=swap_send.at[c], recv_sem=swap_recv.at[c],
            device_id=(w, n + 1 - 2 * half), device_id_type=MESH)

    def swap_start(c):
        settled[c] = passing[c, 3] + passing[CHUNKS + c, 2] + masked[chunk_rows(c, z), :]
        swap_copy(c).start()

    def spread_copy(t, k):
        way, steps, c = STREAMS[t]
        part = column_ref.at[chunk_rows(c, ring(-way * k))]
        return pltpu.make_async_remote_copy(
            src_ref=part, dst_ref=part, send_sem=spread_send.at[t, k], recv_sem=spread_recv.at[t, k],
            device_id=(w, beside(t)), device_id_type=MESH)

    def spread_step(k):
        for t, (way, steps, c) in enumerate(STREAMS):
            if k < steps:
                spread_copy(t, k).wait()
            if k + 1 < steps:
                spread_copy(t, k + 1).start()

    mat_copy = pltpu.make_async_copy(mat_ref, mats, small_sem.at[0])
    slab_copy = pltpu.make_async_copy(slab_ref, masked, small_sem.at[1])
    mat_halo_copy = pltpu.make_async_remote_copy(
        src_ref=mat_ref.at[:, layers - 1], dst_ref=mat_halo, send_sem=mat_send, recv_sem=mat_recv,
        device_id=(w, group(1)), device_id_type=MESH)

    slab_copy.start()
    mat_copy.start()
    for sc in range(6):
        load(sc).start()

    barrier = pltpu.get_barrier_semaphore()

    def greet(d, carry):
        pl.semaphore_signal(barrier, inc=1, device_id=(w, group(d)), device_id_type=MESH)
        pl.semaphore_signal(barrier, inc=1, device_id=(across(d), n), device_id_type=MESH)
        return carry

    lax.fori_loop(1, count, greet, 0)
    mine = jnp.where(owner_ref[0] == n, 1.0, 0.0).astype(BF16)
    slab_copy.wait()

    def mask(q, carry):
        part = pl.ds(pl.multiple_of(q * piece_rows, piece_rows), piece_rows)
        masked[part, :] = masked[part, :] * mine
        return carry

    lax.fori_loop(0, RING, mask, 0)
    pl.semaphore_wait(barrier, 2 * (count - 1))

    mat_halo_copy.start()
    for sc in range(6):
        halo_copy(sc).start()
    for t in range(len(STREAMS)):
        ring_start(t)

    acc[...] = jnp.zeros_like(acc)
    late[...] = jnp.zeros_like(late)
    right[...] = jnp.zeros_like(right)
    pieces[...] = jnp.zeros_like(pieces)

    table = table_ref[...].astype(F32)
    mat_copy.wait()
    mat_halo_copy.wait()
    bottom = jnp.where(n == 0, 0.0, 1.0)
    top = jnp.where(n == count - 1, 1.0, 0.0)

    def lame(material):
        shear = jnp.zeros(material.shape, F32)
        dilate = jnp.zeros(material.shape, F32)
        for k in range(table.shape[1]):
            hit = material == k
            shear = jnp.where(hit, table[0:1, k:k + 1], shear)
            dilate = jnp.where(hit, table[1:2, k:k + 1], dilate)
        return shear, dilate

    for s in range(2):
        below = [x * bottom for x in lame(mat_halo[s])]
        cells = [lame(mats[s, i]) for i in range(layers)]
        for i in range(layers):
            here = cells[i]
            lower_x = below if i == 0 else cells[i - 1]

            def weights(other):
                m = 0.5 * (here[0] + other[0])
                return m, m + (m + 0.5 * (here[1] + other[1]))

            x_low = weights(lower_x)
            if i + 1 < layers:
                x_high = weights(cells[i + 1])
            else:
                x_high = [x * top for x in weights((jnp.zeros_like(here[0]),) * 2)]
            y_low = weights([shift_up(x, 0) for x in here])
            y_high = weights([shift_down(x, 0) for x in here])
            z_low = weights([shift_up(x, 1) for x in here])
            z_high = weights([shift_down(x, 1) for x in here])
            lane = lax.broadcasted_iota(jnp.int32, here[0].shape, 1)
            for c in range(3):
                px, py, pz = (int(c == d) for d in range(3))
                coef[3 * s + c, i, 0] = (x_low[px] + x_high[px]) + (y_low[py] + y_high[py]) + (z_low[pz] + z_high[pz])
                coef[3 * s + c, i, 1] = x_low[px]
                coef[3 * s + c, i, 2] = y_low[py]
                coef[3 * s + c, i, 3] = jnp.where(lane == 0, 0.0, z_low[pz])
                coef[3 * s + c, i, 4] = jnp.where(lane == lane.shape[1] - 1, 0.0, z_high[pz])
                if i == 0:
                    coef_halo[3 * s + c] = x_low[px] * bottom

    rows_y = 8

    def interior(sc, carry):
        s = lax.div(sc, 3)
        load(sc).wait()
        for i in range(layers):
            natural[i] = tiles[sc, :, i].astype(F32).reshape(funcs * rows_y, 128)

        def field(i, y):
            return natural[i, pl.ds(y, funcs, stride=rows_y), :]

        def k(i, which, y):
            return coef[sc, i, which, pl.ds(y, 1), :]

        for i in range(layers):
            for y in range(rows_y):
                v = field(i, y)
                image = k(i, 0, y) * v
                if i > 0:
                    image = image - k(i, 1, y) * field(i - 1, y)
                if i + 1 < layers:
                    image = image - k(i + 1, 1, y) * field(i + 1, y)
                if y > 0:
                    image = image - k(i, 2, y) * field(i, y - 1)
                if y + 1 < rows_y:
                    image = image - k(i, 2, y + 1) * field(i, y + 1)
                image = image - k(i, 3, y) * pltpu.roll(v, 1, 1) - k(i, 4, y) * pltpu.roll(v, 127, 1)
                lanes = slice(128 * y, 128 * (y + 1))
                hi, lo = split2(image)
                vb = v.astype(BF16)
                left[:, lanes] = vb
                if i == 0:
                    first[sc, :, lanes] = vb
                right[0:funcs, lanes] = hi
                right[128:128 + funcs, lanes] = lo
            acc[s] += lax.dot_general(left[...], right[...], NT, preferred_element_type=F32)

        @pl.when((sc >= 1) & (sc <= 2))
        def _():
            for t in range(len(STREAMS)):
                ring_step(t, sc - 1, False)

        @pl.when(sc == 3)
        def _():
            for t in range(CHUNKS):
                ring_step(t, 2, False)
            for t in range(CHUNKS, 2 * CHUNKS):
                ring_step(t, 2, True)

        @pl.when(sc == 4)
        def _():
            for c in range(CHUNKS):
                ring_step(c, 3, True)
                swap_start(c)

        return carry

    lax.fori_loop(0, 6, interior, 0)
    for c in range(CHUNKS):
        swap_copy(c).wait()
        column_ref[chunk_rows(c, z), :] = settled[c] + swapped[c]
        for t in (c, CHUNKS + c):
            spread_copy(t, 0).start()

    def boundary(sc, carry):
        s = lax.div(sc, 3)
        halo_copy(sc).wait()
        natural[0] = halo[sc].astype(F32).reshape(funcs * rows_y, 128)
        for y in range(rows_y):
            h = natural[0, pl.ds(y, funcs, stride=rows_y), :]
            hi, lo = split2(coef_halo[sc, pl.ds(y, 1), :] * h)
            lanes = slice(128 * y, 128 * (y + 1))
            left[:, lanes] = h.astype(BF16)
            right[0:funcs, lanes] = hi
            right[128:128 + funcs, lanes] = lo
        late[s, 0:funcs] += lax.dot_general(left[...], right[...], NT, preferred_element_type=F32)
        late[s, funcs:2 * funcs] += lax.dot_general(first[sc], right[...], NT, preferred_element_type=F32)
        return carry

    lax.fori_loop(0, 4, boundary, 0)
    spread_step(0)
    lax.fori_loop(4, 6, boundary, 0)

    head = masked[0:128, :].astype(F32)
    for q in range(16):
        pieces[q, 16:24, :] = head[8 * q:8 * (q + 1), :]
    for s in range(2):
        both = acc[s] + late[s, 0:funcs]
        total = both[:, 0:128] + both[:, 128:256]
        cross = late[s, funcs:2 * funcs, 0:128] + late[s, funcs:2 * funcs, 128:256]
        square = jnp.concatenate([cross, jnp.zeros((128 - funcs, 128), F32)], 0)
        total = total - cross - square.T[0:funcs]
        for part in range(RING):
            pieces[2 * part + s, 0:12, :] = total[12 * part:12 * (part + 1), :]

    def rs_copy(d):
        return pltpu.make_async_remote_copy(
            src_ref=pieces.at[group(d)], dst_ref=landed.at[n], send_sem=rs_send.at[d], recv_sem=rs_recv.at[d],
            device_id=(w, group(d)), device_id_type=MESH)

    def wide_copy(d):
        return pltpu.make_async_remote_copy(
            src_ref=reduced, dst_ref=wide_in.at[w], send_sem=wide_send.at[d], recv_sem=wide_recv.at[d],
            device_id=(across(d), n), device_id_type=MESH)

    def own_copy(d):
        return pltpu.make_async_remote_copy(
            src_ref=reduced, dst_ref=own_ref.at[n], send_sem=own_send.at[d], recv_sem=own_recv.at[d],
            device_id=(w, group(d)), device_id_type=MESH)

    def panel_copy(d):
        return pltpu.make_async_remote_copy(
            src_ref=chosen.at[group(d)], dst_ref=panel_ref.at[n], send_sem=panel_send.at[d], recv_sem=panel_recv.at[d],
            device_id=(w, group(d)), device_id_type=MESH)

    def start_all(copy):
        lax.fori_loop(1, count, lambda d, carry: (copy(d).start(), carry)[1], 0)

    def wait_all(copy):
        lax.fori_loop(1, count, lambda d, carry: (copy(d).wait(), carry)[1], 0)

    start_all(rs_copy)
    landed[n] = pieces[n]
    spread_step(1)
    wait_all(rs_copy)
    total = landed[0]
    for q in range(1, 16):
        total = total + landed[q]
    reduced[...] = total
    reduced[12:14, :] = jnp.full((2, 128), -1.0, F32)
    reduced[12:14, 0:funcs] = ids_ref[...].astype(F32)
    start_all(wide_copy)
    own_ref[n] = reduced[...]
    wide_in[w] = reduced[...]
    spread_step(2)
    wait_all(wide_copy)
    of_owner = wide_in[owner_ref[0]]
    for q in range(16):
        chosen[q, 0:24, :] = of_owner
        chosen[q, 24:32, :] = wide_in[q, 16:24, :]
    start_all(panel_copy)
    start_all(own_copy)
    panel_ref[n] = chosen[n]
    spread_step(3)
    wait_all(panel_copy)
    wait_all(own_copy)


def gather(owner, table, ids, basis, mat, slab):
    subs, funcs, comps, layers, rows_y, depth = basis.shape
    vmem, anyspace = pl.BlockSpec(memory_space=pltpu.VMEM), pl.BlockSpec(memory_space=pl.ANY)
    dma = pltpu.SemaphoreType.DMA
    piece = jax.ShapeDtypeStruct((16, PIECE, 128), F32)
    wider = jax.ShapeDtypeStruct((16, WIDER, 128), F32)
    chunk = slab.shape[0] // RING // CHUNKS
    streams = len(STREAMS)
    return pl.pallas_call(
        gather_kernel,
        out_shape=(piece, wider, jax.ShapeDtypeStruct(slab.shape, BF16)),
        in_specs=[pl.BlockSpec(memory_space=pltpu.SMEM), vmem, vmem, anyspace, anyspace, anyspace],
        out_specs=(vmem, vmem, vmem),
        scratch_shapes=[
            pltpu.VMEM((6, funcs, layers, rows_y, depth), BF16),
            pltpu.VMEM((6, funcs, rows_y, depth), BF16),
            pltpu.VMEM((subs, layers, rows_y, depth), jnp.int32),
            pltpu.VMEM((subs, rows_y, depth), jnp.int32),
            pltpu.VMEM((6, layers, 5, rows_y, depth), F32),
            pltpu.VMEM((6, rows_y, depth), F32),
            pltpu.VMEM((layers, funcs * rows_y, depth), F32),
            pltpu.VMEM((funcs, rows_y * depth), BF16),
            pltpu.VMEM((256, rows_y * depth), BF16),
            pltpu.VMEM((6, funcs, rows_y * depth), BF16),
            pltpu.VMEM((subs, funcs, 256), F32),
            pltpu.VMEM((subs, 2 * funcs, 256), F32),
            pltpu.VMEM((16, PIECE, 128), F32),
            pltpu.VMEM((16, PIECE, 128), F32),
            pltpu.VMEM((PIECE, 128), F32),
            pltpu.VMEM((16, PIECE, 128), F32),
            pltpu.VMEM((16, WIDER, 128), F32),
            pltpu.VMEM(slab.shape, BF16),
            pltpu.VMEM((streams, 4, chunk, 128), BF16),
            pltpu.VMEM((CHUNKS, chunk, 128), BF16),
            pltpu.VMEM((CHUNKS, chunk, 128), BF16),
            dma((6,)), dma((2,)), dma((6,)), dma((6,)), dma, dma,
            dma((16,)), dma((16,)), dma((16,)), dma((16,)), dma((16,)), dma((16,)), dma((16,)), dma((16,)),
            dma((streams, 4)), dma((streams, 4)), dma((CHUNKS,)), dma((CHUNKS,)), dma((streams, 4)), dma((streams, 4)),
        ],
        compiler_params=pltpu.CompilerParams(collective_id=0, has_side_effects=True, vmem_limit_bytes=63 << 20),
        name="galerkin_gather",
    )(owner, table, ids, basis, mat, slab)


def panel_kernel(
    owner_ref, panel_hbm, own_hbm, column_hbm, slab_hbm, out_ref, galerkin_ref,
    panel_ref, own_ref, column_ref, slab_ref, block, added_own, lower, parts, rows_bf, load_sem,
):
    w, n = lax.axis_index("wide"), lax.axis_index("narrow")
    owner = owner_ref[0]
    pairs = ((panel_hbm, panel_ref), (own_hbm, own_ref), (column_hbm, column_ref), (slab_hbm, slab_ref))
    loads = [pltpu.make_async_copy(src, dst, load_sem.at[q]) for q, (src, dst) in enumerate(pairs)]
    for copy in loads:
        copy.start()
    funcs = galerkin_ref.shape[1]
    height, tile = out_ref.shape[0], 512

    def slots(pieces_ref, s):
        ids = pieces_ref[0, 12 + s:13 + s, :]
        index = lax.broadcasted_iota(jnp.int32, (128, 128), 0).astype(F32)
        return jnp.where(index == ids, 1.0, 0.0)

    def added_of(pieces_ref):
        total = jnp.zeros((128, 128), F32)
        for s in range(2):
            place = slots(pieces_ref, s)
            for z in range(8):
                block[12 * z:12 * (z + 1), :] = pieces_ref[2 * z + s, 0:12, :]
            total = total + exact_dot(exact_dot(place, block[...], NN), place, NT)
        return total

    block[...] = jnp.zeros_like(block)
    loads[0].wait()
    diagonal = added_of(panel_ref) + jnp.concatenate([panel_ref[q, 16:24, :] for q in range(16)], 0)
    diagonal = 0.5 * (diagonal + diagonal.T)
    sub = lax.broadcasted_iota(jnp.int32, (8, 128), 0)
    lane = lax.broadcasted_iota(jnp.int32, (8, 128), 1)
    a = [diagonal[8 * b:8 * (b + 1)] for b in range(16)]
    m = [jnp.where(lane == sub + 8 * b, 1.0, 0.0) for b in range(16)]
    for j in range(128):
        b0, r = divmod(j, 8)
        row_a, row_m = a[b0][r:r + 1], m[b0][r:r + 1]
        inverse = 1.0 / row_a[:, j:j + 1]
        row_a, row_m = row_a * inverse, row_m * inverse
        for b in range(b0, 16):
            if b == b0 and r == 7:
                continue
            f = a[b][:, j:j + 1]
            if b == b0:
                f = jnp.where(sub[:, 0:1] > r, f, 0.0)
            a[b] = a[b] - f * row_a
            m[b] = m[b] - f * row_m
    upper = []
    for b in range(16):
        on_diagonal = lane == sub + 8 * b
        d = jnp.sum(jnp.where(on_diagonal, a[b], 0.0), axis=1, keepdims=True)
        scale = lax.rsqrt(d)
        upper.append(jnp.where(lane >= sub + 8 * b, a[b] * scale, 0.0))
        m[b] = m[b] * scale
    lower[...] = jnp.concatenate(upper, 0).T
    inverse = jnp.concatenate(m, 0)
    hi, rest = split2(inverse)
    mid, low = split2(inverse - hi.astype(F32))
    parts[0:128] = hi
    parts[128:256] = mid
    parts[256:384] = low

    def solve(x):
        y = lax.dot_general(x, parts[...], NT, preferred_element_type=F32)
        return y[:, 0:128] + (y[:, 128:256] + y[:, 256:384])

    loads[1].wait()
    for s in range(2):
        for z in range(8):
            galerkin_ref[s, 12 * z:12 * (z + 1), :] = own_ref[2 * z + s, 0:12, 0:funcs]
    loads[2].wait()
    loads[3].wait()
    rows = jnp.concatenate([panel_ref[q, 24:32, :] for q in range(16)], 0)
    rows_bf[...] = solve(rows.astype(BF16)).astype(BF16)
    added_own[...] = jnp.zeros_like(added_own)

    @pl.when((w == n) & (n >= owner))
    def _():
        added_own[...] = added_of(own_ref)

    def store(start, size, factor, base):
        part = pl.ds(start, size)

        @pl.when(n > owner)
        def _():
            update = lax.dot_general(factor, rows_bf[...], NT, preferred_element_type=F32)
            out_ref[part, :] = (base - update).astype(BF16)

        @pl.when(n == owner)
        def _():
            out_ref[part, :] = factor

        @pl.when(n < owner)
        def _():
            out_ref[part, :] = base.astype(BF16)

    solved = solve(column_ref[0:128, :])
    solved = jnp.where(w == owner, lower[...], solved)
    solved = jnp.where(w < owner, 0.0, solved)
    store(0, 128, solved.astype(BF16), slab_ref[0:128, :].astype(F32) + added_own[...])

    def body(t, carry):
        start = pl.multiple_of(128 + t * tile, 128)
        part = pl.ds(start, tile)
        store(start, tile, solve(column_ref[part, :]).astype(BF16), slab_ref[part, :].astype(F32))
        return carry

    steps = (height - 128) // tile
    lax.fori_loop(0, steps, body, 0)
    done = 128 + steps * tile
    rest = slice(done, height)
    store(done, height - done, solve(column_ref[rest, :]).astype(BF16), slab_ref[rest, :].astype(F32))


def panel_step(owner, panel, own, column, slab, funcs):
    vmem = pl.BlockSpec(memory_space=pltpu.VMEM)
    return pl.pallas_call(
        panel_kernel,
        out_shape=(jax.ShapeDtypeStruct(slab.shape, BF16), jax.ShapeDtypeStruct((2, funcs, funcs), F32)),
        in_specs=[pl.BlockSpec(memory_space=pltpu.SMEM)] + [pl.BlockSpec(memory_space=pl.ANY)] * 4,
        out_specs=(vmem, vmem),
        scratch_shapes=[
            pltpu.VMEM(panel.shape, F32), pltpu.VMEM(own.shape, F32), pltpu.VMEM(slab.shape, BF16), pltpu.VMEM(slab.shape, BF16),
            pltpu.VMEM((128, 128), F32), pltpu.VMEM((128, 128), F32), pltpu.VMEM((128, 128), F32),
            pltpu.VMEM((384, 128), BF16), pltpu.VMEM((128, 128), BF16),
            pltpu.SemaphoreType.DMA((4,)),
        ],
        compiler_params=pltpu.CompilerParams(vmem_limit_bytes=63 << 20),
        name="panel_step",
    )(owner, panel, own, column, slab)


def on_device(coarse_basis, material_ids, lame_table, coarse_ids, coarse_slab, panel_owner):
    own, panel, column = gather(panel_owner, lame_table, coarse_ids, coarse_basis, material_ids, coarse_slab)
    return panel_step(panel_owner, panel, own, column, coarse_slab, coarse_basis.shape[1])


def solution(mesh):
    return jax.shard_map(
        on_device,
        mesh=mesh,
        in_specs=(
            P("wide", None, None, "narrow", None, None),
            P("wide", "narrow", None, None),
            P(),
            P("wide", None),
            P("wide", "narrow"),
            P(),
        ),
        out_specs=(P("wide", "narrow"), P("wide", None, None)),
        check_vma=False,
    )
```

```python
import functools

import jax
import jax.numpy as jnp
from jax import lax
from jax.experimental import pallas as pl
from jax.experimental.pallas import tpu as pltpu
from jax.sharding import PartitionSpec as P

MESH = pl.DeviceIdType.MESH
F32, BF16 = jnp.float32, jnp.bfloat16
NT = (((1,), (1,)), ((), ()))
NN = (((1,), (0,)), ((), ()))
PIECE = 24
WIDER = 32
RING = 8
CHUNKS = 2
SUMS = ((-1, 6, 0), (-1, 6, 1), (1, 1, 0), (1, 1, 1))
SPREAD = ((-1, 4, 0), (-1, 4, 1), (1, 3, 0), (1, 3, 1))


def exact_dot(a, b, dims):
    return lax.dot_general(a, b, dims, precision=lax.Precision.HIGHEST, preferred_element_type=F32)


def split2(x):
    hi = x.astype(BF16)
    return hi, (x - hi.astype(F32)).astype(BF16)


def shift_up(x, axis):
    index = lax.broadcasted_iota(jnp.int32, x.shape, axis)
    return jnp.where(index == 0, 0.0, pltpu.roll(x, 1, axis))


def shift_down(x, axis):
    size = x.shape[axis]
    index = lax.broadcasted_iota(jnp.int32, x.shape, axis)
    return jnp.where(index == size - 1, 0.0, pltpu.roll(x, size - 1, axis))


def gather_kernel(
    owner_ref, table_ref, ids_ref, basis_ref, mat_ref, slab_ref,
    own_ref, panel_ref, column_ref,
    tiles, halo, mats, mat_halo, coef, coef_halo, natural, left, right, first, acc, late,
    pieces, landed, reduced, wide_in, chosen, masked, passing, settled, swapped,
    load_sem, small_sem, halo_send, halo_recv, mat_send, mat_recv, rs_send, rs_recv,
    wide_send, wide_recv, own_send, own_recv, panel_send, panel_recv,
    ring_send, ring_recv, swap_send, swap_recv, spread_send, spread_recv,
):
    w, n = lax.axis_index("wide"), lax.axis_index("narrow")
    count = lax.axis_size("narrow")
    funcs = basis_ref.shape[1]
    layers = basis_ref.shape[3]
    group = lambda d: lax.rem(n + d, count)
    across = lambda d: lax.rem(w + d, count)

    def load(sc):
        s, c = lax.div(sc, 3), lax.rem(sc, 3)
        return pltpu.make_async_copy(basis_ref.at[s, :, c], tiles.at[sc], load_sem.at[sc])

    def halo_copy(sc):
        s, c = lax.div(sc, 3), lax.rem(sc, 3)
        return pltpu.make_async_remote_copy(
            src_ref=basis_ref.at[s, :, c, layers - 1], dst_ref=halo.at[sc],
            send_sem=halo_send.at[sc], recv_sem=halo_recv.at[sc],
            device_id=(w, group(1)), device_id_type=MESH)

    z, half = lax.div(n, 2), lax.rem(n, 2)
    piece_rows = column_ref.shape[0] // RING
    chunk = piece_rows // CHUNKS
    ring = lambda shift: lax.rem(z + shift + RING, RING)
    beside = lambda way: 2 * ring(way) + half

    def chunk_rows(c, piece):
        return pl.ds(pl.multiple_of(piece * piece_rows + c * chunk, chunk), chunk)

    def ring_copy(t, k, source=None):
        return pltpu.make_async_remote_copy(
            src_ref=passing.at[t, k - 1] if source is None else source, dst_ref=passing.at[t, k],
            send_sem=ring_send.at[t, k], recv_sem=ring_recv.at[t, k],
            device_id=(w, beside(SUMS[t][0])), device_id_type=MESH)

    def ring_start(t):
        way, steps, c = SUMS[t]
        ring_copy(t, 0, masked.at[chunk_rows(c, ring(way * steps))]).start()

    def ring_step(t, k, last):
        way, steps, c = SUMS[t]
        ring_copy(t, k, passing.at[t, k]).wait()
        if not last:
            passing[t, k] += masked[chunk_rows(c, ring(way * (steps - 1 - k))), :]
            ring_copy(t, k + 1, passing.at[t, k]).start()

    def swap_copy(c):
        return pltpu.make_async_remote_copy(
            src_ref=settled.at[c], dst_ref=swapped.at[c], send_sem=swap_send.at[c], recv_sem=swap_recv.at[c],
            device_id=(w, n + 1 - 2 * half), device_id_type=MESH)

    def swap_start(c):
        settled[c] = passing[c, SUMS[0][1] - 1] + passing[CHUNKS + c, SUMS[2][1] - 1] + masked[chunk_rows(c, z), :]
        swap_copy(c).start()

    def spread_copy(t, k):
        way, steps, c = SPREAD[t]
        part = column_ref.at[chunk_rows(c, ring(-way * k))]
        return pltpu.make_async_remote_copy(
            src_ref=part, dst_ref=part, send_sem=spread_send.at[t, k], recv_sem=spread_recv.at[t, k],
            device_id=(w, beside(way)), device_id_type=MESH)

    def spread_step(k):
        for t, (way, steps, c) in enumerate(SPREAD):
            if k < steps:
                spread_copy(t, k).wait()
            if k + 1 < steps:
                spread_copy(t, k + 1).start()

    mat_copy = pltpu.make_async_copy(mat_ref, mats, small_sem.at[0])
    slab_copy = pltpu.make_async_copy(slab_ref, masked, small_sem.at[1])
    mat_halo_copy = pltpu.make_async_remote_copy(
        src_ref=mat_ref.at[:, layers - 1], dst_ref=mat_halo, send_sem=mat_send, recv_sem=mat_recv,
        device_id=(w, group(1)), device_id_type=MESH)

    slab_copy.start()
    mat_copy.start()
    for sc in range(6):
        load(sc).start()

    barrier = pltpu.get_barrier_semaphore()

    def greet(d, carry):
        pl.semaphore_signal(barrier, inc=1, device_id=(w, group(d)), device_id_type=MESH)
        pl.semaphore_signal(barrier, inc=1, device_id=(across(d), n), device_id_type=MESH)
        return carry

    lax.fori_loop(1, count, greet, 0)
    mine = jnp.where(owner_ref[0] == n, 1.0, 0.0).astype(BF16)
    slab_copy.wait()

    def mask(q, carry):
        part = pl.ds(pl.multiple_of(q * piece_rows, piece_rows), piece_rows)
        masked[part, :] = masked[part, :] * mine
        return carry

    lax.fori_loop(0, RING, mask, 0)
    pl.semaphore_wait(barrier, 2 * (count - 1))

    mat_halo_copy.start()
    for t in range(len(SUMS)):
        ring_start(t)
    for sc in range(2):
        halo_copy(sc).start()

    acc[...] = jnp.zeros_like(acc)
    late[...] = jnp.zeros_like(late)
    right[...] = jnp.zeros_like(right)
    pieces[...] = jnp.zeros_like(pieces)

    table = table_ref[...].astype(F32)
    mat_copy.wait()
    mat_halo_copy.wait()
    bottom = jnp.where(n == 0, 0.0, 1.0)
    top = jnp.where(n == count - 1, 1.0, 0.0)

    def lame(material):
        shear = jnp.zeros(material.shape, F32)
        dilate = jnp.zeros(material.shape, F32)
        for k in range(table.shape[1]):
            hit = material == k
            shear = jnp.where(hit, table[0:1, k:k + 1], shear)
            dilate = jnp.where(hit, table[1:2, k:k + 1], dilate)
        return shear, dilate

    for s in range(2):
        below = [x * bottom for x in lame(mat_halo[s])]
        cells = [lame(mats[s, i]) for i in range(layers)]
        for i in range(layers):
            here = cells[i]
            lower_x = below if i == 0 else cells[i - 1]

            def weights(other):
                m = 0.5 * (here[0] + other[0])
                return m, m + (m + 0.5 * (here[1] + other[1]))

            x_low = weights(lower_x)
            if i + 1 < layers:
                x_high = weights(cells[i + 1])
            else:
                x_high = [x * top for x in weights((jnp.zeros_like(here[0]),) * 2)]
            y_low = weights([shift_up(x, 0) for x in here])
            y_high = weights([shift_down(x, 0) for x in here])
            z_low = weights([shift_up(x, 1) for x in here])
            z_high = weights([shift_down(x, 1) for x in here])
            lane = lax.broadcasted_iota(jnp.int32, here[0].shape, 1)
            for c in range(3):
                px, py, pz = (int(c == d) for d in range(3))
                coef[3 * s + c, i, 0] = (x_low[px] + x_high[px]) + (y_low[py] + y_high[py]) + (z_low[pz] + z_high[pz])
                coef[3 * s + c, i, 1] = x_low[px]
                coef[3 * s + c, i, 2] = y_low[py]
                coef[3 * s + c, i, 3] = jnp.where(lane == 0, 0.0, z_low[pz])
                coef[3 * s + c, i, 4] = jnp.where(lane == lane.shape[1] - 1, 0.0, z_high[pz])
                if i == 0:
                    coef_halo[3 * s + c] = x_low[px] * bottom

    rows_y = 8

    def interior(sc, carry):
        s = lax.div(sc, 3)
        load(sc).wait()
        for i in range(layers):
            natural[i] = tiles[sc, :, i].astype(F32).reshape(funcs * rows_y, 128)

        def field(i, y):
            return natural[i, pl.ds(y, funcs, stride=rows_y), :]

        def k(i, which, y):
            return coef[sc, i, which, pl.ds(y, 1), :]

        for i in range(layers):
            for y in range(rows_y):
                v = field(i, y)
                image = k(i, 0, y) * v
                if i > 0:
                    image = image - k(i, 1, y) * field(i - 1, y)
                if i + 1 < layers:
                    image = image - k(i + 1, 1, y) * field(i + 1, y)
                if y > 0:
                    image = image - k(i, 2, y) * field(i, y - 1)
                if y + 1 < rows_y:
                    image = image - k(i, 2, y + 1) * field(i, y + 1)
                image = image - k(i, 3, y) * pltpu.roll(v, 1, 1) - k(i, 4, y) * pltpu.roll(v, 127, 1)
                lanes = slice(128 * y, 128 * (y + 1))
                hi, lo = split2(image)
                vb = v.astype(BF16)
                left[:, lanes] = vb
                if i == 0:
                    first[sc, :, lanes] = vb
                right[0:funcs, lanes] = hi
                right[128:128 + funcs, lanes] = lo
            acc[s] += lax.dot_general(left[...], right[...], NT, preferred_element_type=F32)
        halo_copy(sc).wait_send()

        @pl.when(sc < 4)
        def _():
            halo_copy(sc + 2).start()

        @pl.when(sc >= 1)
        def _():
            for t in range(CHUNKS):
                ring_step(t, sc - 1, False)

        return carry

    lax.fori_loop(0, 6, interior, 0)
    def boundary(sc, carry):
        s = lax.div(sc, 3)
        halo_copy(sc).wait_recv()
        natural[0] = halo[sc].astype(F32).reshape(funcs * rows_y, 128)
        for y in range(rows_y):
            h = natural[0, pl.ds(y, funcs, stride=rows_y), :]
            hi, lo = split2(coef_halo[sc, pl.ds(y, 1), :] * h)
            lanes = slice(128 * y, 128 * (y + 1))
            left[:, lanes] = h.astype(BF16)
            right[0:funcs, lanes] = hi
            right[128:128 + funcs, lanes] = lo
        late[s, 0:funcs] += lax.dot_general(left[...], right[...], NT, preferred_element_type=F32)
        late[s, funcs:2 * funcs] += lax.dot_general(first[sc], right[...], NT, preferred_element_type=F32)
        return carry

    lax.fori_loop(0, 6, boundary, 0)

    head = masked[0:128, :].astype(F32)
    for q in range(16):
        pieces[q, 16:24, :] = head[8 * q:8 * (q + 1), :]
    for s in range(2):
        both = acc[s] + late[s, 0:funcs]
        total = both[:, 0:128] + both[:, 128:256]
        cross = late[s, funcs:2 * funcs, 0:128] + late[s, funcs:2 * funcs, 128:256]
        square = jnp.concatenate([cross, jnp.zeros((128 - funcs, 128), F32)], 0)
        total = total - cross - square.T[0:funcs]
        for part in range(RING):
            pieces[2 * part + s, 0:12, :] = total[12 * part:12 * (part + 1), :]

    def rs_copy(d):
        return pltpu.make_async_remote_copy(
            src_ref=pieces.at[group(d)], dst_ref=landed.at[n], send_sem=rs_send.at[d], recv_sem=rs_recv.at[d],
            device_id=(w, group(d)), device_id_type=MESH)

    def wide_copy(d):
        return pltpu.make_async_remote_copy(
            src_ref=reduced, dst_ref=wide_in.at[w], send_sem=wide_send.at[d], recv_sem=wide_recv.at[d],
            device_id=(across(d), n), device_id_type=MESH)

    def own_copy(d):
        return pltpu.make_async_remote_copy(
            src_ref=reduced, dst_ref=own_ref.at[n], send_sem=own_send.at[d], recv_sem=own_recv.at[d],
            device_id=(w, group(d)), device_id_type=MESH)

    def panel_copy(d):
        return pltpu.make_async_remote_copy(
            src_ref=chosen.at[group(d)], dst_ref=panel_ref.at[n], send_sem=panel_send.at[d], recv_sem=panel_recv.at[d],
            device_id=(w, group(d)), device_id_type=MESH)

    def start_all(copy):
        lax.fori_loop(1, count, lambda d, carry: (copy(d).start(), carry)[1], 0)

    def wait_all(copy):
        lax.fori_loop(1, count, lambda d, carry: (copy(d).wait(), carry)[1], 0)

    start_all(rs_copy)
    landed[n] = pieces[n]
    for c in range(CHUNKS):
        ring_step(c, SUMS[0][1] - 1, True)
        ring_step(CHUNKS + c, 0, True)
        swap_start(c)
    wait_all(rs_copy)
    total = landed[0]
    for q in range(1, 16):
        total = total + landed[q]
    reduced[...] = total
    reduced[12:14, :] = jnp.full((2, 128), -1.0, F32)
    reduced[12:14, 0:funcs] = ids_ref[...].astype(F32)
    start_all(wide_copy)
    start_all(own_copy)
    own_ref[n] = reduced[...]
    wide_in[w] = reduced[...]
    for c in range(CHUNKS):
        swap_copy(c).wait()
        column_ref[chunk_rows(c, z), :] = settled[c] + swapped[c]
        for t in (c, CHUNKS + c):
            spread_copy(t, 0).start()
    wait_all(wide_copy)
    of_owner = wide_in[owner_ref[0]]
    for q in range(16):
        chosen[q, 0:24, :] = of_owner
        chosen[q, 24:32, :] = wide_in[q, 16:24, :]
    start_all(panel_copy)
    panel_ref[n] = chosen[n]
    for k in range(4):
        spread_step(k)
    wait_all(panel_copy)
    wait_all(own_copy)


def gather(owner, table, ids, basis, mat, slab):
    subs, funcs, comps, layers, rows_y, depth = basis.shape
    vmem, anyspace = pl.BlockSpec(memory_space=pltpu.VMEM), pl.BlockSpec(memory_space=pl.ANY)
    dma = pltpu.SemaphoreType.DMA
    piece = jax.ShapeDtypeStruct((16, PIECE, 128), F32)
    wider = jax.ShapeDtypeStruct((16, WIDER, 128), F32)
    chunk = slab.shape[0] // RING // CHUNKS
    streams, longest = len(SUMS), max(steps for _, steps, _ in SUMS)
    return pl.pallas_call(
        gather_kernel,
        out_shape=(piece, wider, jax.ShapeDtypeStruct(slab.shape, BF16)),
        in_specs=[pl.BlockSpec(memory_space=pltpu.SMEM), vmem, vmem, anyspace, anyspace, anyspace],
        out_specs=(vmem, vmem, vmem),
        scratch_shapes=[
            pltpu.VMEM((6, funcs, layers, rows_y, depth), BF16),
            pltpu.VMEM((6, funcs, rows_y, depth), BF16),
            pltpu.VMEM((subs, layers, rows_y, depth), jnp.int32),
            pltpu.VMEM((subs, rows_y, depth), jnp.int32),
            pltpu.VMEM((6, layers, 5, rows_y, depth), F32),
            pltpu.VMEM((6, rows_y, depth), F32),
            pltpu.VMEM((layers, funcs * rows_y, depth), F32),
            pltpu.VMEM((funcs, rows_y * depth), BF16),
            pltpu.VMEM((256, rows_y * depth), BF16),
            pltpu.VMEM((6, funcs, rows_y * depth), BF16),
            pltpu.VMEM((subs, funcs, 256), F32),
            pltpu.VMEM((subs, 2 * funcs, 256), F32),
            pltpu.VMEM((16, PIECE, 128), F32),
            pltpu.VMEM((16, PIECE, 128), F32),
            pltpu.VMEM((PIECE, 128), F32),
            pltpu.VMEM((16, PIECE, 128), F32),
            pltpu.VMEM((16, WIDER, 128), F32),
            pltpu.VMEM(slab.shape, BF16),
            pltpu.VMEM((streams, longest, chunk, 128), BF16),
            pltpu.VMEM((CHUNKS, chunk, 128), BF16),
            pltpu.VMEM((CHUNKS, chunk, 128), BF16),
            dma((6,)), dma((2,)), dma((6,)), dma((6,)), dma, dma,
            dma((16,)), dma((16,)), dma((16,)), dma((16,)), dma((16,)), dma((16,)), dma((16,)), dma((16,)),
            dma((streams, longest)), dma((streams, longest)), dma((CHUNKS,)), dma((CHUNKS,)), dma((streams, 4)), dma((streams, 4)),
        ],
        compiler_params=pltpu.CompilerParams(collective_id=0, has_side_effects=True, vmem_limit_bytes=63 << 20),
        name="galerkin_gather",
    )(owner, table, ids, basis, mat, slab)


def panel_kernel(
    owner_ref, panel_hbm, own_hbm, column_hbm, slab_hbm, out_ref, galerkin_ref,
    panel_ref, own_ref, column_ref, slab_ref, block, added_own, lower, parts, rows_bf, load_sem,
):
    w, n = lax.axis_index("wide"), lax.axis_index("narrow")
    owner = owner_ref[0]
    pairs = ((panel_hbm, panel_ref), (own_hbm, own_ref), (column_hbm, column_ref), (slab_hbm, slab_ref))
    loads = [pltpu.make_async_copy(src, dst, load_sem.at[q]) for q, (src, dst) in enumerate(pairs)]
    for copy in loads:
        copy.start()
    funcs = galerkin_ref.shape[1]
    height, tile = out_ref.shape[0], 512

    def slots(pieces_ref, s):
        ids = pieces_ref[0, 12 + s:13 + s, :]
        index = lax.broadcasted_iota(jnp.int32, (128, 128), 0).astype(F32)
        return jnp.where(index == ids, 1.0, 0.0)

    def added_of(pieces_ref):
        total = jnp.zeros((128, 128), F32)
        for s in range(2):
            place = slots(pieces_ref, s)
            for z in range(8):
                block[12 * z:12 * (z + 1), :] = pieces_ref[2 * z + s, 0:12, :]
            total = total + exact_dot(exact_dot(place, block[...], NN), place, NT)
        return total

    block[...] = jnp.zeros_like(block)
    loads[0].wait()
    diagonal = added_of(panel_ref) + jnp.concatenate([panel_ref[q, 16:24, :] for q in range(16)], 0)
    diagonal = 0.5 * (diagonal + diagonal.T)
    sub = lax.broadcasted_iota(jnp.int32, (8, 128), 0)
    lane = lax.broadcasted_iota(jnp.int32, (8, 128), 1)
    a = [diagonal[8 * b:8 * (b + 1)] for b in range(16)]
    m = [jnp.where(lane == sub + 8 * b, 1.0, 0.0) for b in range(16)]
    for j in range(128):
        b0, r = divmod(j, 8)
        row_a, row_m = a[b0][r:r + 1], m[b0][r:r + 1]
        inverse = 1.0 / row_a[:, j:j + 1]
        row_a, row_m = row_a * inverse, row_m * inverse
        for b in range(b0, 16):
            if b == b0 and r == 7:
                continue
            f = a[b][:, j:j + 1]
            if b == b0:
                f = jnp.where(sub[:, 0:1] > r, f, 0.0)
            a[b] = a[b] - f * row_a
            m[b] = m[b] - f * row_m
    upper = []
    for b in range(16):
        on_diagonal = lane == sub + 8 * b
        d = jnp.sum(jnp.where(on_diagonal, a[b], 0.0), axis=1, keepdims=True)
        scale = lax.rsqrt(d)
        upper.append(jnp.where(lane >= sub + 8 * b, a[b] * scale, 0.0))
        m[b] = m[b] * scale
    lower[...] = jnp.concatenate(upper, 0).T
    inverse = jnp.concatenate(m, 0)
    hi, rest = split2(inverse)
    mid, low = split2(inverse - hi.astype(F32))
    parts[0:128] = hi
    parts[128:256] = mid
    parts[256:384] = low

    def solve(x):
        y = lax.dot_general(x, parts[...], NT, preferred_element_type=F32)
        return y[:, 0:128] + (y[:, 128:256] + y[:, 256:384])

    loads[1].wait()
    for s in range(2):
        for z in range(8):
            galerkin_ref[s, 12 * z:12 * (z + 1), :] = own_ref[2 * z + s, 0:12, 0:funcs]
    loads[2].wait()
    loads[3].wait()
    rows = jnp.concatenate([panel_ref[q, 24:32, :] for q in range(16)], 0)
    rows_bf[...] = solve(rows.astype(BF16)).astype(BF16)
    added_own[...] = jnp.zeros_like(added_own)

    @pl.when((w == n) & (n >= owner))
    def _():
        added_own[...] = added_of(own_ref)

    def store(start, size, factor, base):
        part = pl.ds(start, size)

        @pl.when(n > owner)
        def _():
            update = lax.dot_general(factor, rows_bf[...], NT, preferred_element_type=F32)
            out_ref[part, :] = (base - update).astype(BF16)

        @pl.when(n == owner)
        def _():
            out_ref[part, :] = factor

        @pl.when(n < owner)
        def _():
            out_ref[part, :] = base.astype(BF16)

    solved = solve(column_ref[0:128, :])
    solved = jnp.where(w == owner, lower[...], solved)
    solved = jnp.where(w < owner, 0.0, solved)
    store(0, 128, solved.astype(BF16), slab_ref[0:128, :].astype(F32) + added_own[...])

    def body(t, carry):
        start = pl.multiple_of(128 + t * tile, 128)
        part = pl.ds(start, tile)
        store(start, tile, solve(column_ref[part, :]).astype(BF16), slab_ref[part, :].astype(F32))
        return carry

    steps = (height - 128) // tile
    lax.fori_loop(0, steps, body, 0)
    done = 128 + steps * tile
    rest = slice(done, height)
    store(done, height - done, solve(column_ref[rest, :]).astype(BF16), slab_ref[rest, :].astype(F32))


def panel_step(owner, panel, own, column, slab, funcs):
    vmem = pl.BlockSpec(memory_space=pltpu.VMEM)
    return pl.pallas_call(
        panel_kernel,
        out_shape=(jax.ShapeDtypeStruct(slab.shape, BF16), jax.ShapeDtypeStruct((2, funcs, funcs), F32)),
        in_specs=[pl.BlockSpec(memory_space=pltpu.SMEM)] + [pl.BlockSpec(memory_space=pl.ANY)] * 4,
        out_specs=(vmem, vmem),
        scratch_shapes=[
            pltpu.VMEM(panel.shape, F32), pltpu.VMEM(own.shape, F32), pltpu.VMEM(slab.shape, BF16), pltpu.VMEM(slab.shape, BF16),
            pltpu.VMEM((128, 128), F32), pltpu.VMEM((128, 128), F32), pltpu.VMEM((128, 128), F32),
            pltpu.VMEM((384, 128), BF16), pltpu.VMEM((128, 128), BF16),
            pltpu.SemaphoreType.DMA((4,)),
        ],
        compiler_params=pltpu.CompilerParams(vmem_limit_bytes=63 << 20),
        name="panel_step",
    )(owner, panel, own, column, slab)


def on_device(coarse_basis, material_ids, lame_table, coarse_ids, coarse_slab, panel_owner):
    own, panel, column = gather(panel_owner, lame_table, coarse_ids, coarse_basis, material_ids, coarse_slab)
    return panel_step(panel_owner, panel, own, column, coarse_slab, coarse_basis.shape[1])


def solution(mesh):
    return jax.shard_map(
        on_device,
        mesh=mesh,
        in_specs=(
            P("wide", None, None, "narrow", None, None),
            P("wide", "narrow", None, None),
            P(),
            P("wide", None),
            P("wide", "narrow"),
            P(),
        ),
        out_specs=(P("wide", "narrow"), P("wide", None, None)),
        check_vma=False,
    )
```

```python
import functools

import jax
import jax.numpy as jnp
from jax import lax
from jax.experimental import pallas as pl
from jax.experimental.pallas import tpu as pltpu
from jax.sharding import PartitionSpec as P

MESH = pl.DeviceIdType.MESH
F32, BF16 = jnp.float32, jnp.bfloat16
NT = (((1,), (1,)), ((), ()))
NN = (((1,), (0,)), ((), ()))
PIECE = 24
WIDER = 32
RING = 8
TILES = 8
CHUNKS = 2
SUMS = ((-1, 6, 0), (-1, 6, 1), (1, 1, 0), (1, 1, 1))
SPREAD = ((-1, 4, 0), (-1, 4, 1), (1, 3, 0), (1, 3, 1))


def exact_dot(a, b, dims):
    return lax.dot_general(a, b, dims, precision=lax.Precision.HIGHEST, preferred_element_type=F32)


def split2(x):
    hi = x.astype(BF16)
    return hi, (x - hi.astype(F32)).astype(BF16)


def shift_up(x, axis):
    index = lax.broadcasted_iota(jnp.int32, x.shape, axis)
    return jnp.where(index == 0, 0.0, pltpu.roll(x, 1, axis))


def shift_down(x, axis):
    size = x.shape[axis]
    index = lax.broadcasted_iota(jnp.int32, x.shape, axis)
    return jnp.where(index == size - 1, 0.0, pltpu.roll(x, size - 1, axis))


def added_of(pieces_ref, block):
    total = jnp.zeros((128, 128), F32)
    index = lax.broadcasted_iota(jnp.int32, (128, 128), 0).astype(F32)
    for s in range(2):
        place = jnp.where(index == pieces_ref[0, 12 + s:13 + s, :], 1.0, 0.0)
        for part in range(RING):
            block[12 * part:12 * (part + 1), :] = pieces_ref[2 * part + s, 0:12, :]
        total = total + exact_dot(exact_dot(place, block[...], NN), place, NT)
    return total


def solve(x, parts):
    y = lax.dot_general(x, parts, NT, preferred_element_type=F32)
    return y[:, 0:128] + (y[:, 128:256] + y[:, 256:384])


def gather_kernel(
    owner_ref, table_ref, ids_ref, basis_ref, mat_ref, slab_ref,
    own_ref, column_ref, parts_ref, lower_ref, rows_ref,
    tiles, halo, mats, mat_halo, coef, coef_halo, natural, left, right, first, acc, late,
    pieces, landed, reduced, wide_in, chosen, panel_ref, block, masked, passing, settled, swapped,
    load_sem, small_sem, halo_send, halo_recv, mat_send, mat_recv, rs_send, rs_recv,
    wide_send, wide_recv, own_send, own_recv, panel_send, panel_recv,
    ring_send, ring_recv, swap_send, swap_recv, spread_send, spread_recv,
):
    w, n = lax.axis_index("wide"), lax.axis_index("narrow")
    count = lax.axis_size("narrow")
    funcs = basis_ref.shape[1]
    layers = basis_ref.shape[3]
    group = lambda d: lax.rem(n + d, count)
    across = lambda d: lax.rem(w + d, count)

    def load(sc):
        s, c = lax.div(sc, 3), lax.rem(sc, 3)
        return pltpu.make_async_copy(basis_ref.at[s, :, c], tiles.at[sc], load_sem.at[sc])

    def halo_copy(sc):
        s, c = lax.div(sc, 3), lax.rem(sc, 3)
        return pltpu.make_async_remote_copy(
            src_ref=basis_ref.at[s, :, c, layers - 1], dst_ref=halo.at[sc],
            send_sem=halo_send.at[sc], recv_sem=halo_recv.at[sc],
            device_id=(w, group(1)), device_id_type=MESH)

    z, half = lax.div(n, 2), lax.rem(n, 2)
    piece_rows = column_ref.shape[0] // RING
    chunk = piece_rows // CHUNKS
    ring = lambda shift: lax.rem(z + shift + RING, RING)
    beside = lambda way: 2 * ring(way) + half

    def chunk_rows(c, piece):
        return pl.ds(pl.multiple_of(piece * piece_rows + c * chunk, chunk), chunk)

    def ring_copy(t, k, source=None):
        return pltpu.make_async_remote_copy(
            src_ref=passing.at[t, k - 1] if source is None else source, dst_ref=passing.at[t, k],
            send_sem=ring_send.at[t, k], recv_sem=ring_recv.at[t, k],
            device_id=(w, beside(SUMS[t][0])), device_id_type=MESH)

    def ring_start(t):
        way, steps, c = SUMS[t]
        ring_copy(t, 0, masked.at[chunk_rows(c, ring(way * steps))]).start()

    def ring_step(t, k, last):
        way, steps, c = SUMS[t]
        ring_copy(t, k, passing.at[t, k]).wait()
        if not last:
            passing[t, k] += masked[chunk_rows(c, ring(way * (steps - 1 - k))), :]
            ring_copy(t, k + 1, passing.at[t, k]).start()

    def swap_copy(c):
        return pltpu.make_async_remote_copy(
            src_ref=settled.at[c], dst_ref=swapped.at[c], send_sem=swap_send.at[c], recv_sem=swap_recv.at[c],
            device_id=(w, n + 1 - 2 * half), device_id_type=MESH)

    def swap_start(c):
        settled[c] = passing[c, SUMS[0][1] - 1] + passing[CHUNKS + c, SUMS[2][1] - 1] + masked[chunk_rows(c, z), :]
        swap_copy(c).start()

    def spread_copy(t, k):
        way, steps, c = SPREAD[t]
        part = column_ref.at[chunk_rows(c, ring(-way * k))]
        return pltpu.make_async_remote_copy(
            src_ref=part, dst_ref=part, send_sem=spread_send.at[t, k], recv_sem=spread_recv.at[t, k],
            device_id=(w, beside(way)), device_id_type=MESH)

    def spread_step(k):
        for t, (way, steps, c) in enumerate(SPREAD):
            if k < steps:
                spread_copy(t, k).wait()
            if k + 1 < steps:
                spread_copy(t, k + 1).start()

    mat_copy = pltpu.make_async_copy(mat_ref, mats, small_sem.at[0])
    slab_copy = pltpu.make_async_copy(slab_ref, masked, small_sem.at[1])
    mat_halo_copy = pltpu.make_async_remote_copy(
        src_ref=mat_ref.at[:, layers - 1], dst_ref=mat_halo, send_sem=mat_send, recv_sem=mat_recv,
        device_id=(w, group(1)), device_id_type=MESH)

    slab_copy.start()
    mat_copy.start()
    for sc in range(6):
        load(sc).start()

    barrier = pltpu.get_barrier_semaphore()

    def greet(d, carry):
        pl.semaphore_signal(barrier, inc=1, device_id=(w, group(d)), device_id_type=MESH)
        pl.semaphore_signal(barrier, inc=1, device_id=(across(d), n), device_id_type=MESH)
        return carry

    lax.fori_loop(1, count, greet, 0)
    mine = jnp.where(owner_ref[0] == n, 1.0, 0.0).astype(BF16)
    slab_copy.wait()

    def mask(q, carry):
        part = pl.ds(pl.multiple_of(q * piece_rows, piece_rows), piece_rows)
        masked[part, :] = masked[part, :] * mine
        return carry

    lax.fori_loop(0, RING, mask, 0)
    pl.semaphore_wait(barrier, 2 * (count - 1))

    mat_halo_copy.start()
    for t in range(len(SUMS)):
        ring_start(t)
    for sc in range(2):
        halo_copy(sc).start()

    acc[...] = jnp.zeros_like(acc)
    late[...] = jnp.zeros_like(late)
    right[...] = jnp.zeros_like(right)
    pieces[...] = jnp.zeros_like(pieces)

    table = table_ref[...].astype(F32)
    mat_copy.wait()
    mat_halo_copy.wait()
    bottom = jnp.where(n == 0, 0.0, 1.0)
    top = jnp.where(n == count - 1, 1.0, 0.0)

    def lame(material):
        shear = jnp.zeros(material.shape, F32)
        dilate = jnp.zeros(material.shape, F32)
        for k in range(table.shape[1]):
            hit = material == k
            shear = jnp.where(hit, table[0:1, k:k + 1], shear)
            dilate = jnp.where(hit, table[1:2, k:k + 1], dilate)
        return shear, dilate

    for s in range(2):
        below = [x * bottom for x in lame(mat_halo[s])]
        cells = [lame(mats[s, i]) for i in range(layers)]
        for i in range(layers):
            here = cells[i]
            lower_x = below if i == 0 else cells[i - 1]

            def weights(other):
                m = 0.5 * (here[0] + other[0])
                return m, m + (m + 0.5 * (here[1] + other[1]))

            x_low = weights(lower_x)
            if i + 1 < layers:
                x_high = weights(cells[i + 1])
            else:
                x_high = [x * top for x in weights((jnp.zeros_like(here[0]),) * 2)]
            y_low = weights([shift_up(x, 0) for x in here])
            y_high = weights([shift_down(x, 0) for x in here])
            z_low = weights([shift_up(x, 1) for x in here])
            z_high = weights([shift_down(x, 1) for x in here])
            lane = lax.broadcasted_iota(jnp.int32, here[0].shape, 1)
            for c in range(3):
                px, py, pz = (int(c == d) for d in range(3))
                coef[3 * s + c, i, 0] = (x_low[px] + x_high[px]) + (y_low[py] + y_high[py]) + (z_low[pz] + z_high[pz])
                coef[3 * s + c, i, 1] = x_low[px]
                coef[3 * s + c, i, 2] = y_low[py]
                coef[3 * s + c, i, 3] = jnp.where(lane == 0, 0.0, z_low[pz])
                coef[3 * s + c, i, 4] = jnp.where(lane == lane.shape[1] - 1, 0.0, z_high[pz])
                if i == 0:
                    coef_halo[3 * s + c] = x_low[px] * bottom

    rows_y = 8

    def interior(sc, carry):
        s = lax.div(sc, 3)
        load(sc).wait()
        for i in range(layers):
            natural[i] = tiles[sc, :, i].astype(F32).reshape(funcs * rows_y, 128)

        def field(i, y):
            return natural[i, pl.ds(y, funcs, stride=rows_y), :]

        def k(i, which, y):
            return coef[sc, i, which, pl.ds(y, 1), :]

        for i in range(layers):
            for y in range(rows_y):
                v = field(i, y)
                image = k(i, 0, y) * v
                if i > 0:
                    image = image - k(i, 1, y) * field(i - 1, y)
                if i + 1 < layers:
                    image = image - k(i + 1, 1, y) * field(i + 1, y)
                if y > 0:
                    image = image - k(i, 2, y) * field(i, y - 1)
                if y + 1 < rows_y:
                    image = image - k(i, 2, y + 1) * field(i, y + 1)
                image = image - k(i, 3, y) * pltpu.roll(v, 1, 1) - k(i, 4, y) * pltpu.roll(v, 127, 1)
                lanes = slice(128 * y, 128 * (y + 1))
                hi, lo = split2(image)
                vb = v.astype(BF16)
                left[:, lanes] = vb
                if i == 0:
                    first[sc, :, lanes] = vb
                right[0:funcs, lanes] = hi
                right[128:128 + funcs, lanes] = lo
            acc[s] += lax.dot_general(left[...], right[...], NT, preferred_element_type=F32)
        halo_copy(sc).wait_send()

        @pl.when(sc < 4)
        def _():
            halo_copy(sc + 2).start()

        @pl.when(sc >= 1)
        def _():
            for t in range(CHUNKS):
                ring_step(t, sc - 1, False)

        return carry

    lax.fori_loop(0, 6, interior, 0)
    def boundary(sc, carry):
        s = lax.div(sc, 3)
        halo_copy(sc).wait_recv()
        natural[0] = halo[sc].astype(F32).reshape(funcs * rows_y, 128)
        for y in range(rows_y):
            h = natural[0, pl.ds(y, funcs, stride=rows_y), :]
            hi, lo = split2(coef_halo[sc, pl.ds(y, 1), :] * h)
            lanes = slice(128 * y, 128 * (y + 1))
            left[:, lanes] = h.astype(BF16)
            right[0:funcs, lanes] = hi
            right[128:128 + funcs, lanes] = lo
        late[s, 0:funcs] += lax.dot_general(left[...], right[...], NT, preferred_element_type=F32)
        late[s, funcs:2 * funcs] += lax.dot_general(first[sc], right[...], NT, preferred_element_type=F32)
        return carry

    lax.fori_loop(0, 6, boundary, 0)

    head = masked[0:128, :].astype(F32)
    for q in range(16):
        pieces[q, 16:24, :] = head[8 * q:8 * (q + 1), :]
    for s in range(2):
        both = acc[s] + late[s, 0:funcs]
        total = both[:, 0:128] + both[:, 128:256]
        cross = late[s, funcs:2 * funcs, 0:128] + late[s, funcs:2 * funcs, 128:256]
        square = jnp.concatenate([cross, jnp.zeros((128 - funcs, 128), F32)], 0)
        total = total - cross - square.T[0:funcs]
        for part in range(RING):
            pieces[2 * part + s, 0:12, :] = total[12 * part:12 * (part + 1), :]

    def rs_copy(d):
        return pltpu.make_async_remote_copy(
            src_ref=pieces.at[group(d)], dst_ref=landed.at[n], send_sem=rs_send.at[d], recv_sem=rs_recv.at[d],
            device_id=(w, group(d)), device_id_type=MESH)

    def wide_copy(d):
        return pltpu.make_async_remote_copy(
            src_ref=reduced, dst_ref=wide_in.at[w], send_sem=wide_send.at[d], recv_sem=wide_recv.at[d],
            device_id=(across(d), n), device_id_type=MESH)

    def own_copy(d):
        return pltpu.make_async_remote_copy(
            src_ref=reduced, dst_ref=own_ref.at[n], send_sem=own_send.at[d], recv_sem=own_recv.at[d],
            device_id=(w, group(d)), device_id_type=MESH)

    def panel_copy(d):
        return pltpu.make_async_remote_copy(
            src_ref=chosen.at[group(d)], dst_ref=panel_ref.at[n], send_sem=panel_send.at[d], recv_sem=panel_recv.at[d],
            device_id=(w, group(d)), device_id_type=MESH)

    def start_all(copy):
        lax.fori_loop(1, count, lambda d, carry: (copy(d).start(), carry)[1], 0)

    def wait_all(copy):
        lax.fori_loop(1, count, lambda d, carry: (copy(d).wait(), carry)[1], 0)

    start_all(rs_copy)
    landed[n] = pieces[n]
    for c in range(CHUNKS):
        ring_step(c, SUMS[0][1] - 1, True)
        ring_step(CHUNKS + c, 0, True)
        swap_start(c)
    wait_all(rs_copy)
    total = landed[0]
    for q in range(1, 16):
        total = total + landed[q]
    reduced[...] = total
    reduced[12:14, :] = jnp.full((2, 128), -1.0, F32)
    reduced[12:14, 0:funcs] = ids_ref[...].astype(F32)
    start_all(wide_copy)
    start_all(own_copy)
    own_ref[n] = reduced[...]
    wide_in[w] = reduced[...]
    for c in range(CHUNKS):
        swap_copy(c).wait()
        column_ref[chunk_rows(c, z), :] = settled[c] + swapped[c]
        for t in (c, CHUNKS + c):
            spread_copy(t, 0).start()
    wait_all(wide_copy)
    of_owner = wide_in[owner_ref[0]]
    for q in range(16):
        chosen[q, 0:24, :] = of_owner
        chosen[q, 24:32, :] = wide_in[q, 16:24, :]
    start_all(panel_copy)
    panel_ref[n] = chosen[n]
    block[...] = jnp.zeros_like(block)
    spread_step(0)
    spread_step(1)
    wait_all(panel_copy)

    diagonal = added_of(panel_ref, block) + jnp.concatenate([panel_ref[q, 16:24, :] for q in range(16)], 0)
    diagonal = 0.5 * (diagonal + diagonal.T)
    sub = lax.broadcasted_iota(jnp.int32, (8, 128), 0)
    lane = lax.broadcasted_iota(jnp.int32, (8, 128), 1)
    a = [diagonal[8 * b:8 * (b + 1)] for b in range(16)]
    m = [jnp.where(lane == sub + 8 * b, 1.0, 0.0) for b in range(16)]
    for j in range(128):
        if j == 64:
            spread_step(2)
        b0, r = divmod(j, 8)
        row_a, row_m = a[b0][r:r + 1], m[b0][r:r + 1]
        inverse = 1.0 / row_a[:, j:j + 1]
        row_a, row_m = row_a * inverse, row_m * inverse
        for b in range(b0, 16):
            if b == b0 and r == 7:
                continue
            f = a[b][:, j:j + 1]
            if b == b0:
                f = jnp.where(sub[:, 0:1] > r, f, 0.0)
            a[b] = a[b] - f * row_a
            m[b] = m[b] - f * row_m
    upper = []
    for b in range(16):
        on_diagonal = lane == sub + 8 * b
        d = jnp.sum(jnp.where(on_diagonal, a[b], 0.0), axis=1, keepdims=True)
        scale = lax.rsqrt(d)
        upper.append(jnp.where(lane >= sub + 8 * b, a[b] * scale, 0.0))
        m[b] = m[b] * scale
    lower_ref[...] = jnp.concatenate(upper, 0).T
    inverse = jnp.concatenate(m, 0)
    hi, rest = split2(inverse)
    mid, low = split2(inverse - hi.astype(F32))
    parts_ref[0:128] = hi
    parts_ref[128:256] = mid
    parts_ref[256:384] = low

    rows = jnp.concatenate([panel_ref[q, 24:32, :] for q in range(16)], 0)
    rows_ref[...] = solve(rows.astype(BF16), parts_ref[...]).astype(BF16)
    spread_step(3)
    wait_all(own_copy)


def gather(owner, table, ids, basis, mat, slab):
    subs, funcs, comps, layers, rows_y, depth = basis.shape
    vmem, anyspace = pl.BlockSpec(memory_space=pltpu.VMEM), pl.BlockSpec(memory_space=pl.ANY)
    dma = pltpu.SemaphoreType.DMA
    piece = jax.ShapeDtypeStruct((16, PIECE, 128), F32)
    chunk = slab.shape[0] // RING // CHUNKS
    streams, longest = len(SUMS), max(steps for _, steps, _ in SUMS)
    return pl.pallas_call(
        gather_kernel,
        out_shape=(
            piece, jax.ShapeDtypeStruct(slab.shape, BF16), jax.ShapeDtypeStruct((384, 128), BF16),
            jax.ShapeDtypeStruct((128, 128), F32), jax.ShapeDtypeStruct((128, 128), BF16)),
        in_specs=[pl.BlockSpec(memory_space=pltpu.SMEM), vmem, vmem, anyspace, anyspace, anyspace],
        out_specs=(vmem,) * 5,
        scratch_shapes=[
            pltpu.VMEM((6, funcs, layers, rows_y, depth), BF16),
            pltpu.VMEM((6, funcs, rows_y, depth), BF16),
            pltpu.VMEM((subs, layers, rows_y, depth), jnp.int32),
            pltpu.VMEM((subs, rows_y, depth), jnp.int32),
            pltpu.VMEM((6, layers, 5, rows_y, depth), F32),
            pltpu.VMEM((6, rows_y, depth), F32),
            pltpu.VMEM((layers, funcs * rows_y, depth), F32),
            pltpu.VMEM((funcs, rows_y * depth), BF16),
            pltpu.VMEM((256, rows_y * depth), BF16),
            pltpu.VMEM((6, funcs, rows_y * depth), BF16),
            pltpu.VMEM((subs, funcs, 256), F32),
            pltpu.VMEM((subs, 2 * funcs, 256), F32),
            pltpu.VMEM((16, PIECE, 128), F32),
            pltpu.VMEM((16, PIECE, 128), F32),
            pltpu.VMEM((PIECE, 128), F32),
            pltpu.VMEM((16, PIECE, 128), F32),
            pltpu.VMEM((16, WIDER, 128), F32),
            pltpu.VMEM((16, WIDER, 128), F32),
            pltpu.VMEM((128, 128), F32),
            pltpu.VMEM(slab.shape, BF16),
            pltpu.VMEM((streams, longest, chunk, 128), BF16),
            pltpu.VMEM((CHUNKS, chunk, 128), BF16),
            pltpu.VMEM((CHUNKS, chunk, 128), BF16),
            dma((6,)), dma((2,)), dma((6,)), dma((6,)), dma, dma,
            dma((16,)), dma((16,)), dma((16,)), dma((16,)), dma((16,)), dma((16,)), dma((16,)), dma((16,)),
            dma((streams, longest)), dma((streams, longest)), dma((CHUNKS,)), dma((CHUNKS,)), dma((streams, 4)), dma((streams, 4)),
        ],
        compiler_params=pltpu.CompilerParams(collective_id=0, has_side_effects=True, vmem_limit_bytes=63 << 20),
        name="galerkin_gather",
    )(owner, table, ids, basis, mat, slab)


def panel_kernel(
    owner_ref, own_ref, parts_ref, lower_ref, rows_ref, column_hbm, slab_hbm, out_hbm, galerkin_ref,
    column, slab, out, block, column_sem, slab_sem, out_sem,
):
    w, n = lax.axis_index("wide"), lax.axis_index("narrow")
    owner = owner_ref[0]
    funcs = galerkin_ref.shape[1]
    tile = out.shape[0] // TILES

    def rows_of(t):
        return pl.ds(pl.multiple_of(t * tile, tile), tile)

    def column_load(t):
        return pltpu.make_async_copy(column_hbm.at[rows_of(t)], column.at[rows_of(t)], column_sem.at[t])

    def slab_load(t):
        return pltpu.make_async_copy(slab_hbm.at[rows_of(t)], slab.at[rows_of(t)], slab_sem.at[t])

    def out_store(t):
        return pltpu.make_async_copy(out.at[rows_of(t)], out_hbm.at[rows_of(t)], out_sem.at[t])

    for t in range(TILES):
        column_load(t).start()
        slab_load(t).start()
    block[...] = jnp.zeros_like(block)
    for s in range(2):
        for part in range(RING):
            galerkin_ref[s, 12 * part:12 * (part + 1), :] = own_ref[2 * part + s, 0:12, 0:funcs]

    def store(t, factor):
        part = rows_of(t)

        @pl.when(n > owner)
        def _():
            update = lax.dot_general(factor, rows_ref[...], NT, preferred_element_type=F32)
            out[part, :] = (slab[part, :].astype(F32) - update).astype(BF16)

        @pl.when(n == owner)
        def _():
            out[part, :] = factor

        @pl.when(n < owner)
        def _():
            out[part, :] = slab[part, :]

    column_load(0).wait()
    slab_load(0).wait()
    solved = solve(column[0:tile, :], parts_ref[...])
    top = jnp.where(w == owner, lower_ref[...], solved[0:128])
    top = jnp.where(w < owner, 0.0, top)
    factor = jnp.concatenate([top, solved[128:tile]], 0).astype(BF16)
    store(0, factor)

    @pl.when((w == n) & (n > owner))
    def _():
        update = lax.dot_general(factor[0:128], rows_ref[...], NT, preferred_element_type=F32)
        base = slab[0:128, :].astype(F32) + added_of(own_ref, block)
        out[0:128, :] = (base - update).astype(BF16)

    out_store(0).start()

    def body(t, carry):
        column_load(t).wait()
        slab_load(t).wait()
        store(t, solve(column[rows_of(t), :], parts_ref[...]).astype(BF16))
        out_store(t).start()
        return carry

    lax.fori_loop(1, TILES, body, 0)
    for t in range(TILES):
        out_store(t).wait()


def panel_step(owner, own, column, parts, lower, rows, slab, funcs):
    vmem, anyspace = pl.BlockSpec(memory_space=pltpu.VMEM), pl.BlockSpec(memory_space=pl.ANY)
    dma = pltpu.SemaphoreType.DMA
    return pl.pallas_call(
        panel_kernel,
        out_shape=(jax.ShapeDtypeStruct(slab.shape, BF16), jax.ShapeDtypeStruct((2, funcs, funcs), F32)),
        in_specs=[pl.BlockSpec(memory_space=pltpu.SMEM), vmem, vmem, vmem, vmem, anyspace, anyspace],
        out_specs=(anyspace, vmem),
        scratch_shapes=[
            pltpu.VMEM(slab.shape, BF16), pltpu.VMEM(slab.shape, BF16), pltpu.VMEM(slab.shape, BF16),
            pltpu.VMEM((128, 128), F32), dma((TILES,)), dma((TILES,)), dma((TILES,)),
        ],
        compiler_params=pltpu.CompilerParams(vmem_limit_bytes=63 << 20),
        name="panel_step",
    )(owner, own, parts, lower, rows, column, slab)


def on_device(coarse_basis, material_ids, lame_table, coarse_ids, coarse_slab, panel_owner):
    own, column, parts, lower, rows = gather(panel_owner, lame_table, coarse_ids, coarse_basis, material_ids, coarse_slab)
    return panel_step(panel_owner, own, column, parts, lower, rows, coarse_slab, coarse_basis.shape[1])


def solution(mesh):
    return jax.shard_map(
        on_device,
        mesh=mesh,
        in_specs=(
            P("wide", None, None, "narrow", None, None),
            P("wide", "narrow", None, None),
            P(),
            P("wide", None),
            P("wide", "narrow"),
            P(),
        ),
        out_specs=(P("wide", "narrow"), P("wide", None, None)),
        check_vma=False,
    )
```

```python
import functools

import jax
import jax.numpy as jnp
from jax import lax
from jax.experimental import pallas as pl
from jax.experimental.pallas import tpu as pltpu
from jax.sharding import PartitionSpec as P

MESH = pl.DeviceIdType.MESH
F32, BF16 = jnp.float32, jnp.bfloat16
NT = (((1,), (1,)), ((), ()))
NN = (((1,), (0,)), ((), ()))
PIECE = 24
WIDER = 32
RING = 8
TILES = 8
CHUNKS = 2
SUMS = ((-1, 4, 0), (-1, 4, 1), (1, 3, 0), (1, 3, 1))
SPREAD = ((-1, 4, 0), (-1, 4, 1), (1, 3, 0), (1, 3, 1))


def exact_dot(a, b, dims):
    return lax.dot_general(a, b, dims, precision=lax.Precision.HIGHEST, preferred_element_type=F32)


def split2(x):
    hi = x.astype(BF16)
    return hi, (x - hi.astype(F32)).astype(BF16)


def shift_up(x, axis):
    index = lax.broadcasted_iota(jnp.int32, x.shape, axis)
    return jnp.where(index == 0, 0.0, pltpu.roll(x, 1, axis))


def shift_down(x, axis):
    size = x.shape[axis]
    index = lax.broadcasted_iota(jnp.int32, x.shape, axis)
    return jnp.where(index == size - 1, 0.0, pltpu.roll(x, size - 1, axis))


def added_of(pieces_ref, block):
    total = jnp.zeros((128, 128), F32)
    index = lax.broadcasted_iota(jnp.int32, (128, 128), 0).astype(F32)
    for s in range(2):
        place = jnp.where(index == pieces_ref[0, 12 + s:13 + s, :], 1.0, 0.0)
        for part in range(RING):
            block[12 * part:12 * (part + 1), :] = pieces_ref[2 * part + s, 0:12, :]
        total = total + exact_dot(exact_dot(place, block[...], NN), place, NT)
    return total


def solve(x, parts):
    y = lax.dot_general(x, parts, NT, preferred_element_type=F32)
    return y[:, 0:128] + (y[:, 128:256] + y[:, 256:384])


def gather_kernel(
    owner_ref, table_ref, ids_ref, basis_ref, mat_ref, slab_ref,
    own_ref, column_ref, parts_ref, lower_ref, rows_ref,
    tiles, halo, mats, mat_halo, coef, coef_halo, natural, left, right, first, acc, late,
    pieces, landed, reduced, wide_in, chosen, panel_ref, block, masked, passing, settled, swapped,
    load_sem, small_sem, halo_send, halo_recv, mat_send, mat_recv, rs_send, rs_recv,
    wide_send, wide_recv, own_send, own_recv, panel_send, panel_recv,
    ring_send, ring_recv, swap_send, swap_recv, spread_send, spread_recv,
):
    w, n = lax.axis_index("wide"), lax.axis_index("narrow")
    count = lax.axis_size("narrow")
    funcs = basis_ref.shape[1]
    layers = basis_ref.shape[3]
    group = lambda d: lax.rem(n + d, count)
    across = lambda d: lax.rem(w + d, count)

    def load(sc):
        s, c = lax.div(sc, 3), lax.rem(sc, 3)
        return pltpu.make_async_copy(basis_ref.at[s, :, c], tiles.at[sc], load_sem.at[sc])

    def halo_copy(sc):
        s, c = lax.div(sc, 3), lax.rem(sc, 3)
        return pltpu.make_async_remote_copy(
            src_ref=basis_ref.at[s, :, c, (layers - 1) * (1 - s)], dst_ref=halo.at[sc],
            send_sem=halo_send.at[sc], recv_sem=halo_recv.at[sc],
            device_id=(w, group(1 + (count - 2) * s)), device_id_type=MESH)

    z, half = lax.div(n, 2), lax.rem(n, 2)
    piece_rows = column_ref.shape[0] // RING
    chunk = piece_rows // CHUNKS
    ring = lambda shift: lax.rem(z + shift + RING, RING)
    flip = 2 * half - 1
    beside = lambda way: 2 * ring(way) + half

    def chunk_rows(c, piece):
        return pl.ds(pl.multiple_of(piece * piece_rows + c * chunk, chunk), chunk)

    def ring_copy(t, k, source=None):
        return pltpu.make_async_remote_copy(
            src_ref=passing.at[t, k - 1] if source is None else source, dst_ref=passing.at[t, k],
            send_sem=ring_send.at[t, k], recv_sem=ring_recv.at[t, k],
            device_id=(w, beside(SUMS[t][0] * flip)), device_id_type=MESH)

    def ring_start(t):
        way, steps, c = SUMS[t]
        way = way * flip
        ring_copy(t, 0, masked.at[chunk_rows(c, ring(way * steps))]).start()

    def ring_step(t, k, last):
        way, steps, c = SUMS[t]
        way = way * flip
        ring_copy(t, k, passing.at[t, k]).wait()
        if not last:
            passing[t, k] += masked[chunk_rows(c, ring(way * (steps - 1 - k))), :]
            ring_copy(t, k + 1, passing.at[t, k]).start()

    def swap_copy(c):
        return pltpu.make_async_remote_copy(
            src_ref=settled.at[c], dst_ref=swapped.at[c], send_sem=swap_send.at[c], recv_sem=swap_recv.at[c],
            device_id=(w, n + 1 - 2 * half), device_id_type=MESH)

    def swap_start(c):
        settled[c] = passing[c, SUMS[0][1] - 1] + passing[CHUNKS + c, SUMS[2][1] - 1] + masked[chunk_rows(c, z), :]
        swap_copy(c).start()

    def spread_copy(t, k):
        way, steps, c = SPREAD[t]
        part = column_ref.at[chunk_rows(c, ring(-way * k))]
        return pltpu.make_async_remote_copy(
            src_ref=part, dst_ref=part, send_sem=spread_send.at[t, k], recv_sem=spread_recv.at[t, k],
            device_id=(w, beside(way)), device_id_type=MESH)

    def spread_step(k):
        for t, (way, steps, c) in enumerate(SPREAD):
            if k < steps:
                spread_copy(t, k).wait()
            if k + 1 < steps:
                spread_copy(t, k + 1).start()

    mat_copy = pltpu.make_async_copy(mat_ref, mats, small_sem.at[0])
    slab_copy = pltpu.make_async_copy(slab_ref, masked, small_sem.at[1])
    def mat_halo_copy(s):
        return pltpu.make_async_remote_copy(
            src_ref=mat_ref.at[s, (layers - 1) * (1 - s)], dst_ref=mat_halo.at[s], send_sem=mat_send.at[s], recv_sem=mat_recv.at[s],
            device_id=(w, group(1 + (count - 2) * s)), device_id_type=MESH)

    slab_copy.start()
    mat_copy.start()
    for sc in range(6):
        load(sc).start()

    barrier = pltpu.get_barrier_semaphore()

    def greet(d, carry):
        pl.semaphore_signal(barrier, inc=1, device_id=(w, group(d)), device_id_type=MESH)
        pl.semaphore_signal(barrier, inc=1, device_id=(across(d), n), device_id_type=MESH)
        return carry

    lax.fori_loop(1, count, greet, 0)
    mine = jnp.where(owner_ref[0] == n, 1.0, 0.0).astype(BF16)
    slab_copy.wait()

    def mask(q, carry):
        part = pl.ds(pl.multiple_of(q * piece_rows, piece_rows), piece_rows)
        masked[part, :] = masked[part, :] * mine
        return carry

    lax.fori_loop(0, RING, mask, 0)
    pl.semaphore_wait(barrier, 2 * (count - 1))

    for s in range(2):
        mat_halo_copy(s).start()
    for t in range(len(SUMS)):
        ring_start(t)
    for sc in range(2):
        halo_copy(sc).start()

    acc[...] = jnp.zeros_like(acc)
    late[...] = jnp.zeros_like(late)
    right[...] = jnp.zeros_like(right)
    pieces[...] = jnp.zeros_like(pieces)

    table = table_ref[...].astype(F32)
    mat_copy.wait()
    for s in range(2):
        mat_halo_copy(s).wait()
    bottom = jnp.where(n == 0, 1.0, 0.0)
    top = jnp.where(n == count - 1, 1.0, 0.0)

    def lame(material):
        shear = jnp.zeros(material.shape, F32)
        dilate = jnp.zeros(material.shape, F32)
        for k in range(table.shape[1]):
            hit = material == k
            shear = jnp.where(hit, table[0:1, k:k + 1], shear)
            dilate = jnp.where(hit, table[1:2, k:k + 1], dilate)
        return shear, dilate

    for s in range(2):
        present = 1.0 - (bottom, top)[s]
        edge, far = (layers - 1) * s, (top, bottom)[s]
        outer = [x * present for x in lame(mat_halo[s])]
        cells = [lame(mats[s, i]) for i in range(layers)]
        for i in range(layers):
            here = cells[i]

            def weights(other):
                m = 0.5 * (here[0] + other[0])
                return m, m + (m + 0.5 * (here[1] + other[1]))

            def outside(owned):
                return weights(outer) if owned else [x * far for x in weights((jnp.zeros_like(here[0]),) * 2)]

            x_low = weights(cells[i - 1]) if i > 0 else outside(s == 0)
            x_high = weights(cells[i + 1]) if i + 1 < layers else outside(s == 1)
            y_low = weights([shift_up(x, 0) for x in here])
            y_high = weights([shift_down(x, 0) for x in here])
            z_low = weights([shift_up(x, 1) for x in here])
            z_high = weights([shift_down(x, 1) for x in here])
            lane = lax.broadcasted_iota(jnp.int32, here[0].shape, 1)
            for c in range(3):
                px, py, pz = (int(c == d) for d in range(3))
                coef[3 * s + c, i, 0] = (x_low[px] + x_high[px]) + (y_low[py] + y_high[py]) + (z_low[pz] + z_high[pz])
                coef[3 * s + c, i, 1] = x_low[px]
                coef[3 * s + c, i, 2] = y_low[py]
                coef[3 * s + c, i, 3] = jnp.where(lane == 0, 0.0, z_low[pz])
                coef[3 * s + c, i, 4] = jnp.where(lane == lane.shape[1] - 1, 0.0, z_high[pz])
                if i == edge:
                    coef_halo[3 * s + c] = (x_low, x_high)[s][px] * present

    rows_y = 8

    def interior(sc, carry):
        s = lax.div(sc, 3)
        load(sc).wait()
        for i in range(layers):
            natural[i] = tiles[sc, :, i].astype(F32).reshape(funcs * rows_y, 128)

        def field(i, y):
            return natural[i, pl.ds(y, funcs, stride=rows_y), :]

        def k(i, which, y):
            return coef[sc, i, which, pl.ds(y, 1), :]

        for i in range(layers):
            for y in range(rows_y):
                v = field(i, y)
                image = k(i, 0, y) * v
                if i > 0:
                    image = image - k(i, 1, y) * field(i - 1, y)
                if i + 1 < layers:
                    image = image - k(i + 1, 1, y) * field(i + 1, y)
                if y > 0:
                    image = image - k(i, 2, y) * field(i, y - 1)
                if y + 1 < rows_y:
                    image = image - k(i, 2, y + 1) * field(i, y + 1)
                image = image - k(i, 3, y) * pltpu.roll(v, 1, 1) - k(i, 4, y) * pltpu.roll(v, 127, 1)
                lanes = slice(128 * y, 128 * (y + 1))
                hi, lo = split2(image)
                vb = v.astype(BF16)
                left[:, lanes] = vb
                right[0:funcs, lanes] = hi
                right[128:128 + funcs, lanes] = lo
            if i in (0, layers - 1):

                @pl.when(s == i // (layers - 1))
                def _():
                    first[sc] = left[...]

            acc[s] += lax.dot_general(left[...], right[...], NT, preferred_element_type=F32)
        halo_copy(sc).wait_send()

        @pl.when(sc < 4)
        def _():
            halo_copy(sc + 2).start()

        @pl.when((sc >= 1) & (sc <= 3))
        def _():
            for t in range(CHUNKS):
                ring_step(t, sc - 1, False)

        @pl.when((sc == 1) | (sc == 2))
        def _():
            for t in range(CHUNKS, 2 * CHUNKS):
                ring_step(t, sc - 1, False)

        return carry

    lax.fori_loop(0, 6, interior, 0)
    def boundary(sc, carry):
        s = lax.div(sc, 3)
        halo_copy(sc).wait_recv()
        natural[0] = halo[sc].astype(F32).reshape(funcs * rows_y, 128)
        for y in range(rows_y):
            h = natural[0, pl.ds(y, funcs, stride=rows_y), :]
            hi, lo = split2(coef_halo[sc, pl.ds(y, 1), :] * h)
            lanes = slice(128 * y, 128 * (y + 1))
            left[:, lanes] = h.astype(BF16)
            right[0:funcs, lanes] = hi
            right[128:128 + funcs, lanes] = lo
        late[s, 0:funcs] += lax.dot_general(left[...], right[...], NT, preferred_element_type=F32)
        late[s, funcs:2 * funcs] += lax.dot_general(first[sc], right[...], NT, preferred_element_type=F32)
        return carry

    for c in range(CHUNKS):
        ring_step(c, SUMS[0][1] - 1, True)
        ring_step(CHUNKS + c, SUMS[2][1] - 1, True)
        swap_start(c)
    lax.fori_loop(0, 6, boundary, 0)

    head = masked[0:128, :].astype(F32)
    for q in range(16):
        pieces[q, 16:24, :] = head[8 * q:8 * (q + 1), :]
    for s in range(2):
        both = acc[s] + late[s, 0:funcs]
        total = both[:, 0:128] + both[:, 128:256]
        cross = late[s, funcs:2 * funcs, 0:128] + late[s, funcs:2 * funcs, 128:256]
        square = jnp.concatenate([cross, jnp.zeros((128 - funcs, 128), F32)], 0)
        total = total - cross - square.T[0:funcs]
        for part in range(RING):
            pieces[2 * part + s, 0:12, :] = total[12 * part:12 * (part + 1), :]

    def rs_copy(d):
        return pltpu.make_async_remote_copy(
            src_ref=pieces.at[group(d)], dst_ref=landed.at[n], send_sem=rs_send.at[d], recv_sem=rs_recv.at[d],
            device_id=(w, group(d)), device_id_type=MESH)

    def wide_copy(d):
        return pltpu.make_async_remote_copy(
            src_ref=reduced, dst_ref=wide_in.at[w], send_sem=wide_send.at[d], recv_sem=wide_recv.at[d],
            device_id=(across(d), n), device_id_type=MESH)

    def own_copy(d):
        return pltpu.make_async_remote_copy(
            src_ref=reduced, dst_ref=own_ref.at[n], send_sem=own_send.at[d], recv_sem=own_recv.at[d],
            device_id=(w, group(d)), device_id_type=MESH)

    def panel_copy(d):
        return pltpu.make_async_remote_copy(
            src_ref=chosen.at[group(d)], dst_ref=panel_ref.at[n], send_sem=panel_send.at[d], recv_sem=panel_recv.at[d],
            device_id=(w, group(d)), device_id_type=MESH)

    def start_all(copy):
        lax.fori_loop(1, count, lambda d, carry: (copy(d).start(), carry)[1], 0)

    def wait_all(copy):
        lax.fori_loop(1, count, lambda d, carry: (copy(d).wait(), carry)[1], 0)

    start_all(rs_copy)
    landed[n] = pieces[n]
    for c in range(CHUNKS):
        swap_copy(c).wait()
        column_ref[chunk_rows(c, z), :] = settled[c] + swapped[c]
        for t in (c, CHUNKS + c):
            spread_copy(t, 0).start()
    wait_all(rs_copy)
    total = landed[0]
    for q in range(1, 16):
        total = total + landed[q]
    reduced[...] = total
    reduced[12:14, :] = jnp.full((2, 128), -1.0, F32)
    reduced[12:14, 0:funcs] = ids_ref[...].astype(F32)
    start_all(wide_copy)
    start_all(own_copy)
    own_ref[n] = reduced[...]
    wide_in[w] = reduced[...]
    spread_step(0)
    wait_all(wide_copy)
    of_owner = wide_in[owner_ref[0]]
    for q in range(16):
        chosen[q, 0:24, :] = of_owner
        chosen[q, 24:32, :] = wide_in[q, 16:24, :]
    start_all(panel_copy)
    panel_ref[n] = chosen[n]
    block[...] = jnp.zeros_like(block)
    spread_step(1)
    wait_all(panel_copy)

    diagonal = added_of(panel_ref, block) + jnp.concatenate([panel_ref[q, 16:24, :] for q in range(16)], 0)
    diagonal = 0.5 * (diagonal + diagonal.T)
    sub = lax.broadcasted_iota(jnp.int32, (8, 128), 0)
    lane = lax.broadcasted_iota(jnp.int32, (8, 128), 1)
    a = [diagonal[8 * b:8 * (b + 1)] for b in range(16)]
    m = [jnp.where(lane == sub + 8 * b, 1.0, 0.0) for b in range(16)]
    for j in range(128):
        if j == 64:
            spread_step(2)
        b0, r = divmod(j, 8)
        row_a, row_m = a[b0][r:r + 1], m[b0][r:r + 1]
        inverse = 1.0 / row_a[:, j:j + 1]
        row_a, row_m = row_a * inverse, row_m * inverse
        for b in range(b0, 16):
            if b == b0 and r == 7:
                continue
            f = a[b][:, j:j + 1]
            if b == b0:
                f = jnp.where(sub[:, 0:1] > r, f, 0.0)
            a[b] = a[b] - f * row_a
            m[b] = m[b] - f * row_m
    upper = []
    for b in range(16):
        on_diagonal = lane == sub + 8 * b
        d = jnp.sum(jnp.where(on_diagonal, a[b], 0.0), axis=1, keepdims=True)
        scale = lax.rsqrt(d)
        upper.append(jnp.where(lane >= sub + 8 * b, a[b] * scale, 0.0))
        m[b] = m[b] * scale
    lower_ref[...] = jnp.concatenate(upper, 0).T
    inverse = jnp.concatenate(m, 0)
    hi, rest = split2(inverse)
    mid, low = split2(inverse - hi.astype(F32))
    parts_ref[0:128] = hi
    parts_ref[128:256] = mid
    parts_ref[256:384] = low

    rows = jnp.concatenate([panel_ref[q, 24:32, :] for q in range(16)], 0)
    rows_ref[...] = solve(rows.astype(BF16), parts_ref[...]).astype(BF16)
    spread_step(3)
    wait_all(own_copy)


def gather(owner, table, ids, basis, mat, slab):
    subs, funcs, comps, layers, rows_y, depth = basis.shape
    vmem, anyspace = pl.BlockSpec(memory_space=pltpu.VMEM), pl.BlockSpec(memory_space=pl.ANY)
    dma = pltpu.SemaphoreType.DMA
    piece = jax.ShapeDtypeStruct((16, PIECE, 128), F32)
    chunk = slab.shape[0] // RING // CHUNKS
    streams, longest = len(SUMS), max(steps for _, steps, _ in SUMS)
    return pl.pallas_call(
        gather_kernel,
        out_shape=(
            piece, jax.ShapeDtypeStruct(slab.shape, BF16), jax.ShapeDtypeStruct((384, 128), BF16),
            jax.ShapeDtypeStruct((128, 128), F32), jax.ShapeDtypeStruct((128, 128), BF16)),
        in_specs=[pl.BlockSpec(memory_space=pltpu.SMEM), vmem, vmem, anyspace, anyspace, anyspace],
        out_specs=(vmem,) * 5,
        scratch_shapes=[
            pltpu.VMEM((6, funcs, layers, rows_y, depth), BF16),
            pltpu.VMEM((6, funcs, rows_y, depth), BF16),
            pltpu.VMEM((subs, layers, rows_y, depth), jnp.int32),
            pltpu.VMEM((subs, rows_y, depth), jnp.int32),
            pltpu.VMEM((6, layers, 5, rows_y, depth), F32),
            pltpu.VMEM((6, rows_y, depth), F32),
            pltpu.VMEM((layers, funcs * rows_y, depth), F32),
            pltpu.VMEM((funcs, rows_y * depth), BF16),
            pltpu.VMEM((256, rows_y * depth), BF16),
            pltpu.VMEM((6, funcs, rows_y * depth), BF16),
            pltpu.VMEM((subs, funcs, 256), F32),
            pltpu.VMEM((subs, 2 * funcs, 256), F32),
            pltpu.VMEM((16, PIECE, 128), F32),
            pltpu.VMEM((16, PIECE, 128), F32),
            pltpu.VMEM((PIECE, 128), F32),
            pltpu.VMEM((16, PIECE, 128), F32),
            pltpu.VMEM((16, WIDER, 128), F32),
            pltpu.VMEM((16, WIDER, 128), F32),
            pltpu.VMEM((128, 128), F32),
            pltpu.VMEM(slab.shape, BF16),
            pltpu.VMEM((streams, longest, chunk, 128), BF16),
            pltpu.VMEM((CHUNKS, chunk, 128), BF16),
            pltpu.VMEM((CHUNKS, chunk, 128), BF16),
            dma((6,)), dma((2,)), dma((6,)), dma((6,)), dma((2,)), dma((2,)),
            dma((16,)), dma((16,)), dma((16,)), dma((16,)), dma((16,)), dma((16,)), dma((16,)), dma((16,)),
            dma((streams, longest)), dma((streams, longest)), dma((CHUNKS,)), dma((CHUNKS,)), dma((streams, 4)), dma((streams, 4)),
        ],
        compiler_params=pltpu.CompilerParams(collective_id=0, has_side_effects=True, vmem_limit_bytes=63 << 20),
        name="galerkin_gather",
    )(owner, table, ids, basis, mat, slab)


def panel_kernel(
    owner_ref, own_ref, parts_ref, lower_ref, rows_ref, column_hbm, slab_hbm, out_hbm, galerkin_ref,
    column, slab, out, block, column_sem, slab_sem, out_sem,
):
    w, n = lax.axis_index("wide"), lax.axis_index("narrow")
    owner = owner_ref[0]
    funcs = galerkin_ref.shape[1]
    tile = out.shape[0] // TILES

    def rows_of(t):
        return pl.ds(pl.multiple_of(t * tile, tile), tile)

    def column_load(t):
        return pltpu.make_async_copy(column_hbm.at[rows_of(t)], column.at[rows_of(t)], column_sem.at[t])

    def slab_load(t):
        return pltpu.make_async_copy(slab_hbm.at[rows_of(t)], slab.at[rows_of(t)], slab_sem.at[t])

    def out_store(t):
        return pltpu.make_async_copy(out.at[rows_of(t)], out_hbm.at[rows_of(t)], out_sem.at[t])

    for t in range(TILES):
        column_load(t).start()
        slab_load(t).start()
    block[...] = jnp.zeros_like(block)
    for s in range(2):
        for part in range(RING):
            galerkin_ref[s, 12 * part:12 * (part + 1), :] = own_ref[2 * part + s, 0:12, 0:funcs]

    def store(t, factor):
        part = rows_of(t)

        @pl.when(n > owner)
        def _():
            update = lax.dot_general(factor, rows_ref[...], NT, preferred_element_type=F32)
            out[part, :] = (slab[part, :].astype(F32) - update).astype(BF16)

        @pl.when(n == owner)
        def _():
            out[part, :] = factor

        @pl.when(n < owner)
        def _():
            out[part, :] = slab[part, :]

    column_load(0).wait()
    slab_load(0).wait()
    solved = solve(column[0:tile, :], parts_ref[...])
    top = jnp.where(w == owner, lower_ref[...], solved[0:128])
    top = jnp.where(w < owner, 0.0, top)
    factor = jnp.concatenate([top, solved[128:tile]], 0).astype(BF16)
    store(0, factor)

    @pl.when((w == n) & (n > owner))
    def _():
        update = lax.dot_general(factor[0:128], rows_ref[...], NT, preferred_element_type=F32)
        base = slab[0:128, :].astype(F32) + added_of(own_ref, block)
        out[0:128, :] = (base - update).astype(BF16)

    out_store(0).start()

    def body(t, carry):
        column_load(t).wait()
        slab_load(t).wait()
        store(t, solve(column[rows_of(t), :], parts_ref[...]).astype(BF16))
        out_store(t).start()
        return carry

    lax.fori_loop(1, TILES, body, 0)
    for t in range(TILES):
        out_store(t).wait()


def panel_step(owner, own, column, parts, lower, rows, slab, funcs):
    vmem, anyspace = pl.BlockSpec(memory_space=pltpu.VMEM), pl.BlockSpec(memory_space=pl.ANY)
    dma = pltpu.SemaphoreType.DMA
    return pl.pallas_call(
        panel_kernel,
        out_shape=(jax.ShapeDtypeStruct(slab.shape, BF16), jax.ShapeDtypeStruct((2, funcs, funcs), F32)),
        in_specs=[pl.BlockSpec(memory_space=pltpu.SMEM), vmem, vmem, vmem, vmem, anyspace, anyspace],
        out_specs=(anyspace, vmem),
        scratch_shapes=[
            pltpu.VMEM(slab.shape, BF16), pltpu.VMEM(slab.shape, BF16), pltpu.VMEM(slab.shape, BF16),
            pltpu.VMEM((128, 128), F32), dma((TILES,)), dma((TILES,)), dma((TILES,)),
        ],
        compiler_params=pltpu.CompilerParams(vmem_limit_bytes=63 << 20),
        name="panel_step",
    )(owner, own, parts, lower, rows, column, slab)


def on_device(coarse_basis, material_ids, lame_table, coarse_ids, coarse_slab, panel_owner):
    own, column, parts, lower, rows = gather(panel_owner, lame_table, coarse_ids, coarse_basis, material_ids, coarse_slab)
    return panel_step(panel_owner, own, column, parts, lower, rows, coarse_slab, coarse_basis.shape[1])


def solution(mesh):
    return jax.shard_map(
        on_device,
        mesh=mesh,
        in_specs=(
            P("wide", None, None, "narrow", None, None),
            P("wide", "narrow", None, None),
            P(),
            P("wide", None),
            P("wide", "narrow"),
            P(),
        ),
        out_specs=(P("wide", "narrow"), P("wide", None, None)),
        check_vma=False,
    )
```

```python
import functools

import jax
import jax.numpy as jnp
from jax import lax
from jax.experimental import pallas as pl
from jax.experimental.pallas import tpu as pltpu
from jax.sharding import PartitionSpec as P

MESH = pl.DeviceIdType.MESH
F32, BF16 = jnp.float32, jnp.bfloat16
NT = (((1,), (1,)), ((), ()))
NN = (((1,), (0,)), ((), ()))
PIECE = 24
WIDER = 32
RING = 8
TILES = 8
CHUNKS = 2
SUMS = ((-1, 4, 0), (-1, 4, 1), (1, 3, 0), (1, 3, 1))
SPREAD = ((-1, 4, 0), (-1, 4, 1), (1, 3, 0), (1, 3, 1))


def exact_dot(a, b, dims):
    return lax.dot_general(a, b, dims, precision=lax.Precision.HIGHEST, preferred_element_type=F32)


def split2(x):
    hi = x.astype(BF16)
    return hi, (x - hi.astype(F32)).astype(BF16)


def shift_up(x, axis):
    index = lax.broadcasted_iota(jnp.int32, x.shape, axis)
    return jnp.where(index == 0, 0.0, pltpu.roll(x, 1, axis))


def shift_down(x, axis):
    size = x.shape[axis]
    index = lax.broadcasted_iota(jnp.int32, x.shape, axis)
    return jnp.where(index == size - 1, 0.0, pltpu.roll(x, size - 1, axis))


def added_of(pieces_ref, block):
    total = jnp.zeros((128, 128), F32)
    index = lax.broadcasted_iota(jnp.int32, (128, 128), 0).astype(F32)
    for s in range(2):
        place = jnp.where(index == pieces_ref[0, 12 + s:13 + s, :], 1.0, 0.0)
        for part in range(RING):
            block[12 * part:12 * (part + 1), :] = pieces_ref[2 * part + s, 0:12, :]
        total = total + exact_dot(exact_dot(place, block[...], NN), place, NT)
    return total


def solve(x, parts):
    y = lax.dot_general(x, parts, NT, preferred_element_type=F32)
    return y[:, 0:128] + (y[:, 128:256] + y[:, 256:384])


def gather_kernel(
    owner_ref, table_ref, ids_ref, basis_ref, mat_ref, slab_ref,
    own_ref, column_ref, parts_ref, lower_ref, rows_ref,
    tiles, halo, mats, mat_halo, coef, coef_halo, natural, left, right, first, acc, late,
    pieces, landed, reduced, wide_in, chosen, panel_ref, block, masked, passing, settled, swapped,
    load_sem, small_sem, halo_send, halo_recv, mat_send, mat_recv, rs_send, rs_recv,
    wide_send, wide_recv, own_send, own_recv, panel_send, panel_recv,
    ring_send, ring_recv, swap_send, swap_recv, spread_send, spread_recv,
):
    w, n = lax.axis_index("wide"), lax.axis_index("narrow")
    count = lax.axis_size("narrow")
    funcs = basis_ref.shape[1]
    layers = basis_ref.shape[3]
    group = lambda d: lax.rem(n + d, count)
    across = lambda d: lax.rem(w + d, count)

    def load(sc):
        s, c = lax.div(sc, 3), lax.rem(sc, 3)
        return pltpu.make_async_copy(basis_ref.at[s, :, c], tiles.at[sc], load_sem.at[sc])

    def halo_copy(sc):
        s, c = lax.div(sc, 3), lax.rem(sc, 3)
        return pltpu.make_async_remote_copy(
            src_ref=basis_ref.at[s, :, c, (layers - 1) * (1 - s)], dst_ref=halo.at[sc],
            send_sem=halo_send.at[sc], recv_sem=halo_recv.at[sc],
            device_id=(w, group(1 + (count - 2) * s)), device_id_type=MESH)

    z, half = lax.div(n, 2), lax.rem(n, 2)
    piece_rows = column_ref.shape[0] // RING
    chunk = piece_rows // CHUNKS
    ring = lambda shift: lax.rem(z + shift + RING, RING)
    flip = 2 * half - 1
    beside = lambda way: 2 * ring(way) + half

    def chunk_rows(c, piece):
        return pl.ds(pl.multiple_of(piece * piece_rows + c * chunk, chunk), chunk)

    def ring_copy(t, k, source=None):
        return pltpu.make_async_remote_copy(
            src_ref=passing.at[t, k - 1] if source is None else source, dst_ref=passing.at[t, k],
            send_sem=ring_send.at[t, k], recv_sem=ring_recv.at[t, k],
            device_id=(w, beside(SUMS[t][0] * flip)), device_id_type=MESH)

    def ring_start(t):
        way, steps, c = SUMS[t]
        way = way * flip
        ring_copy(t, 0, masked.at[chunk_rows(c, ring(way * steps))]).start()

    def ring_step(t, k, last):
        way, steps, c = SUMS[t]
        way = way * flip
        ring_copy(t, k, passing.at[t, k]).wait()
        if not last:
            passing[t, k] += masked[chunk_rows(c, ring(way * (steps - 1 - k))), :]
            ring_copy(t, k + 1, passing.at[t, k]).start()

    def swap_copy(c):
        return pltpu.make_async_remote_copy(
            src_ref=settled.at[c], dst_ref=swapped.at[c], send_sem=swap_send.at[c], recv_sem=swap_recv.at[c],
            device_id=(w, n + 1 - 2 * half), device_id_type=MESH)

    def swap_start(c):
        settled[c] = passing[c, SUMS[0][1] - 1] + passing[CHUNKS + c, SUMS[2][1] - 1] + masked[chunk_rows(c, z), :]
        swap_copy(c).start()

    def spread_copy(t, k):
        way, steps, c = SPREAD[t]
        part = column_ref.at[chunk_rows(c, ring(-way * k))]
        return pltpu.make_async_remote_copy(
            src_ref=part, dst_ref=part, send_sem=spread_send.at[t, k], recv_sem=spread_recv.at[t, k],
            device_id=(w, beside(way)), device_id_type=MESH)

    def spread_step(k):
        for t, (way, steps, c) in enumerate(SPREAD):
            if k < steps:
                spread_copy(t, k).wait()
            if k + 1 < steps:
                spread_copy(t, k + 1).start()

    mat_copy = pltpu.make_async_copy(mat_ref, mats, small_sem.at[0])
    slab_copy = pltpu.make_async_copy(slab_ref, masked, small_sem.at[1])
    def mat_halo_copy(s):
        return pltpu.make_async_remote_copy(
            src_ref=mat_ref.at[s, (layers - 1) * (1 - s)], dst_ref=mat_halo.at[s], send_sem=mat_send.at[s], recv_sem=mat_recv.at[s],
            device_id=(w, group(1 + (count - 2) * s)), device_id_type=MESH)

    slab_copy.start()
    mat_copy.start()
    for sc in range(6):
        load(sc).start()

    barrier = pltpu.get_barrier_semaphore()

    def greet(d, carry):
        pl.semaphore_signal(barrier, inc=1, device_id=(w, group(d)), device_id_type=MESH)
        pl.semaphore_signal(barrier, inc=1, device_id=(across(d), n), device_id_type=MESH)
        return carry

    lax.fori_loop(1, count, greet, 0)
    mine = jnp.where(owner_ref[0] == n, 1.0, 0.0).astype(BF16)
    slab_copy.wait()

    def mask(q, carry):
        part = pl.ds(pl.multiple_of(q * piece_rows, piece_rows), piece_rows)
        masked[part, :] = masked[part, :] * mine
        return carry

    lax.fori_loop(0, RING, mask, 0)
    pl.semaphore_wait(barrier, 2 * (count - 1))

    for s in range(2):
        mat_halo_copy(s).start()
    for t in range(len(SUMS)):
        ring_start(t)
    halo_copy(0).start()

    acc[...] = jnp.zeros_like(acc)
    late[...] = jnp.zeros_like(late)
    right[...] = jnp.zeros_like(right)
    pieces[...] = jnp.zeros_like(pieces)

    table = table_ref[...].astype(F32)
    mat_copy.wait()
    for s in range(2):
        mat_halo_copy(s).wait()
    bottom = jnp.where(n == 0, 1.0, 0.0)
    top = jnp.where(n == count - 1, 1.0, 0.0)

    def lame(material):
        shear = jnp.zeros(material.shape, F32)
        dilate = jnp.zeros(material.shape, F32)
        for k in range(table.shape[1]):
            hit = material == k
            shear = jnp.where(hit, table[0:1, k:k + 1], shear)
            dilate = jnp.where(hit, table[1:2, k:k + 1], dilate)
        return shear, dilate

    for s in range(2):
        present = 1.0 - (bottom, top)[s]
        edge, far = (layers - 1) * s, (top, bottom)[s]
        outer = [x * present for x in lame(mat_halo[s])]
        cells = [lame(mats[s, i]) for i in range(layers)]
        for i in range(layers):
            here = cells[i]

            def weights(other):
                m = 0.5 * (here[0] + other[0])
                return m, m + (m + 0.5 * (here[1] + other[1]))

            def outside(owned):
                return weights(outer) if owned else [x * far for x in weights((jnp.zeros_like(here[0]),) * 2)]

            x_low = weights(cells[i - 1]) if i > 0 else outside(s == 0)
            x_high = weights(cells[i + 1]) if i + 1 < layers else outside(s == 1)
            y_low = weights([shift_up(x, 0) for x in here])
            y_high = weights([shift_down(x, 0) for x in here])
            z_low = weights([shift_up(x, 1) for x in here])
            z_high = weights([shift_down(x, 1) for x in here])
            lane = lax.broadcasted_iota(jnp.int32, here[0].shape, 1)
            for c in range(3):
                px, py, pz = (int(c == d) for d in range(3))
                coef[3 * s + c, i, 0] = (x_low[px] + x_high[px]) + (y_low[py] + y_high[py]) + (z_low[pz] + z_high[pz])
                coef[3 * s + c, i, 1] = x_low[px]
                coef[3 * s + c, i, 2] = y_low[py]
                coef[3 * s + c, i, 3] = jnp.where(lane == 0, 0.0, z_low[pz])
                coef[3 * s + c, i, 4] = jnp.where(lane == lane.shape[1] - 1, 0.0, z_high[pz])
                if i == edge:
                    coef_halo[3 * s + c] = (x_low, x_high)[s][px] * present

    rows_y = 8

    def interior(sc, carry):
        s = lax.div(sc, 3)
        load(sc).wait()
        for i in range(layers):
            natural[i] = tiles[sc, :, i].astype(F32).reshape(funcs * rows_y, 128)

        def field(i, y):
            return natural[i, pl.ds(y, funcs, stride=rows_y), :]

        def k(i, which, y):
            return coef[sc, i, which, pl.ds(y, 1), :]

        for i in range(layers):
            for y in range(rows_y):
                v = field(i, y)
                image = k(i, 0, y) * v
                if i > 0:
                    image = image - k(i, 1, y) * field(i - 1, y)
                if i + 1 < layers:
                    image = image - k(i + 1, 1, y) * field(i + 1, y)
                if y > 0:
                    image = image - k(i, 2, y) * field(i, y - 1)
                if y + 1 < rows_y:
                    image = image - k(i, 2, y + 1) * field(i, y + 1)
                image = image - k(i, 3, y) * pltpu.roll(v, 1, 1) - k(i, 4, y) * pltpu.roll(v, 127, 1)
                lanes = slice(128 * y, 128 * (y + 1))
                hi, lo = split2(image)
                vb = v.astype(BF16)
                left[:, lanes] = vb
                right[0:funcs, lanes] = hi
                right[128:128 + funcs, lanes] = lo
            if i in (0, layers - 1):

                @pl.when(s == i // (layers - 1))
                def _():
                    first[sc] = left[...]

            acc[s] += lax.dot_general(left[...], right[...], NT, preferred_element_type=F32)
        halo_copy(sc).wait_send()

        @pl.when(sc < 5)
        def _():
            halo_copy(sc + 1).start()

        @pl.when((sc >= 1) & (sc <= 3))
        def _():
            for t in range(CHUNKS):
                ring_step(t, sc - 1, False)

        @pl.when((sc == 1) | (sc == 2))
        def _():
            for t in range(CHUNKS, 2 * CHUNKS):
                ring_step(t, sc - 1, False)

        return carry

    lax.fori_loop(0, 6, interior, 0)
    def boundary(sc, carry):
        s = lax.div(sc, 3)
        halo_copy(sc).wait_recv()
        natural[0] = halo[sc].astype(F32).reshape(funcs * rows_y, 128)
        for y in range(rows_y):
            h = natural[0, pl.ds(y, funcs, stride=rows_y), :]
            hi, lo = split2(coef_halo[sc, pl.ds(y, 1), :] * h)
            lanes = slice(128 * y, 128 * (y + 1))
            left[:, lanes] = h.astype(BF16)
            right[0:funcs, lanes] = hi
            right[128:128 + funcs, lanes] = lo
        late[s, 0:funcs] += lax.dot_general(left[...], right[...], NT, preferred_element_type=F32)
        late[s, funcs:2 * funcs] += lax.dot_general(first[sc], right[...], NT, preferred_element_type=F32)
        return carry

    for c in range(CHUNKS):
        ring_step(c, SUMS[0][1] - 1, True)
        ring_step(CHUNKS + c, SUMS[2][1] - 1, True)
        swap_start(c)
    lax.fori_loop(0, 6, boundary, 0)

    head = masked[0:128, :].astype(F32)
    for q in range(16):
        pieces[q, 16:24, :] = head[8 * q:8 * (q + 1), :]
    for s in range(2):
        both = acc[s] + late[s, 0:funcs]
        total = both[:, 0:128] + both[:, 128:256]
        cross = late[s, funcs:2 * funcs, 0:128] + late[s, funcs:2 * funcs, 128:256]
        square = jnp.concatenate([cross, jnp.zeros((128 - funcs, 128), F32)], 0)
        total = total - cross - square.T[0:funcs]
        for part in range(RING):
            pieces[2 * part + s, 0:12, :] = total[12 * part:12 * (part + 1), :]

    def rs_copy(d):
        return pltpu.make_async_remote_copy(
            src_ref=pieces.at[group(d)], dst_ref=landed.at[n], send_sem=rs_send.at[d], recv_sem=rs_recv.at[d],
            device_id=(w, group(d)), device_id_type=MESH)

    def wide_copy(d):
        return pltpu.make_async_remote_copy(
            src_ref=reduced, dst_ref=wide_in.at[w], send_sem=wide_send.at[d], recv_sem=wide_recv.at[d],
            device_id=(across(d), n), device_id_type=MESH)

    def own_copy(d):
        return pltpu.make_async_remote_copy(
            src_ref=reduced, dst_ref=own_ref.at[n], send_sem=own_send.at[d], recv_sem=own_recv.at[d],
            device_id=(w, group(d)), device_id_type=MESH)

    def panel_copy(d):
        return pltpu.make_async_remote_copy(
            src_ref=chosen.at[group(d)], dst_ref=panel_ref.at[n], send_sem=panel_send.at[d], recv_sem=panel_recv.at[d],
            device_id=(w, group(d)), device_id_type=MESH)

    def start_all(copy):
        lax.fori_loop(1, count, lambda d, carry: (copy(d).start(), carry)[1], 0)

    def wait_all(copy):
        lax.fori_loop(1, count, lambda d, carry: (copy(d).wait(), carry)[1], 0)

    start_all(rs_copy)
    landed[n] = pieces[n]
    for c in range(CHUNKS):
        swap_copy(c).wait()
        column_ref[chunk_rows(c, z), :] = settled[c] + swapped[c]
        for t in (c, CHUNKS + c):
            spread_copy(t, 0).start()
    wait_all(rs_copy)
    total = landed[0]
    for q in range(1, 16):
        total = total + landed[q]
    reduced[...] = total
    reduced[12:14, :] = jnp.full((2, 128), -1.0, F32)
    reduced[12:14, 0:funcs] = ids_ref[...].astype(F32)
    start_all(wide_copy)
    start_all(own_copy)
    own_ref[n] = reduced[...]
    wide_in[w] = reduced[...]
    spread_step(0)
    wait_all(wide_copy)
    of_owner = wide_in[owner_ref[0]]
    for q in range(16):
        chosen[q, 0:24, :] = of_owner
        chosen[q, 24:32, :] = wide_in[q, 16:24, :]
    start_all(panel_copy)
    panel_ref[n] = chosen[n]
    block[...] = jnp.zeros_like(block)
    spread_step(1)
    wait_all(panel_copy)

    diagonal = added_of(panel_ref, block) + jnp.concatenate([panel_ref[q, 16:24, :] for q in range(16)], 0)
    diagonal = 0.5 * (diagonal + diagonal.T)
    sub = lax.broadcasted_iota(jnp.int32, (8, 128), 0)
    lane = lax.broadcasted_iota(jnp.int32, (8, 128), 1)
    a = [diagonal[8 * b:8 * (b + 1)] for b in range(16)]
    m = [jnp.where(lane == sub + 8 * b, 1.0, 0.0) for b in range(16)]
    for j in range(128):
        if j == 64:
            spread_step(2)
        b0, r = divmod(j, 8)
        row_a, row_m = a[b0][r:r + 1], m[b0][r:r + 1]
        inverse = 1.0 / row_a[:, j:j + 1]
        row_a, row_m = row_a * inverse, row_m * inverse
        for b in range(b0, 16):
            if b == b0 and r == 7:
                continue
            f = a[b][:, j:j + 1]
            if b == b0:
                f = jnp.where(sub[:, 0:1] > r, f, 0.0)
            a[b] = a[b] - f * row_a
            m[b] = m[b] - f * row_m
    upper = []
    for b in range(16):
        on_diagonal = lane == sub + 8 * b
        d = jnp.sum(jnp.where(on_diagonal, a[b], 0.0), axis=1, keepdims=True)
        scale = lax.rsqrt(d)
        upper.append(jnp.where(lane >= sub + 8 * b, a[b] * scale, 0.0))
        m[b] = m[b] * scale
    lower_ref[...] = jnp.concatenate(upper, 0).T
    inverse = jnp.concatenate(m, 0)
    hi, rest = split2(inverse)
    mid, low = split2(inverse - hi.astype(F32))
    parts_ref[0:128] = hi
    parts_ref[128:256] = mid
    parts_ref[256:384] = low

    rows = jnp.concatenate([panel_ref[q, 24:32, :] for q in range(16)], 0)
    rows_ref[...] = solve(rows.astype(BF16), parts_ref[...]).astype(BF16)
    spread_step(3)
    wait_all(own_copy)


def gather(owner, table, ids, basis, mat, slab):
    subs, funcs, comps, layers, rows_y, depth = basis.shape
    vmem, anyspace = pl.BlockSpec(memory_space=pltpu.VMEM), pl.BlockSpec(memory_space=pl.ANY)
    dma = pltpu.SemaphoreType.DMA
    piece = jax.ShapeDtypeStruct((16, PIECE, 128), F32)
    chunk = slab.shape[0] // RING // CHUNKS
    streams, longest = len(SUMS), max(steps for _, steps, _ in SUMS)
    return pl.pallas_call(
        gather_kernel,
        out_shape=(
            piece, jax.ShapeDtypeStruct(slab.shape, BF16), jax.ShapeDtypeStruct((384, 128), BF16),
            jax.ShapeDtypeStruct((128, 128), F32), jax.ShapeDtypeStruct((128, 128), BF16)),
        in_specs=[pl.BlockSpec(memory_space=pltpu.SMEM), vmem, vmem, anyspace, anyspace, anyspace],
        out_specs=(vmem,) * 5,
        scratch_shapes=[
            pltpu.VMEM((6, funcs, layers, rows_y, depth), BF16),
            pltpu.VMEM((6, funcs, rows_y, depth), BF16),
            pltpu.VMEM((subs, layers, rows_y, depth), jnp.int32),
            pltpu.VMEM((subs, rows_y, depth), jnp.int32),
            pltpu.VMEM((6, layers, 5, rows_y, depth), F32),
            pltpu.VMEM((6, rows_y, depth), F32),
            pltpu.VMEM((layers, funcs * rows_y, depth), F32),
            pltpu.VMEM((funcs, rows_y * depth), BF16),
            pltpu.VMEM((256, rows_y * depth), BF16),
            pltpu.VMEM((6, funcs, rows_y * depth), BF16),
            pltpu.VMEM((subs, funcs, 256), F32),
            pltpu.VMEM((subs, 2 * funcs, 256), F32),
            pltpu.VMEM((16, PIECE, 128), F32),
            pltpu.VMEM((16, PIECE, 128), F32),
            pltpu.VMEM((PIECE, 128), F32),
            pltpu.VMEM((16, PIECE, 128), F32),
            pltpu.VMEM((16, WIDER, 128), F32),
            pltpu.VMEM((16, WIDER, 128), F32),
            pltpu.VMEM((128, 128), F32),
            pltpu.VMEM(slab.shape, BF16),
            pltpu.VMEM((streams, longest, chunk, 128), BF16),
            pltpu.VMEM((CHUNKS, chunk, 128), BF16),
            pltpu.VMEM((CHUNKS, chunk, 128), BF16),
            dma((6,)), dma((2,)), dma((6,)), dma((6,)), dma((2,)), dma((2,)),
            dma((16,)), dma((16,)), dma((16,)), dma((16,)), dma((16,)), dma((16,)), dma((16,)), dma((16,)),
            dma((streams, longest)), dma((streams, longest)), dma((CHUNKS,)), dma((CHUNKS,)), dma((streams, 4)), dma((streams, 4)),
        ],
        compiler_params=pltpu.CompilerParams(collective_id=0, has_side_effects=True, vmem_limit_bytes=63 << 20),
        name="galerkin_gather",
    )(owner, table, ids, basis, mat, slab)


def panel_kernel(
    owner_ref, own_ref, parts_ref, lower_ref, rows_ref, column_hbm, slab_hbm, out_hbm, galerkin_ref,
    column, slab, out, block, column_sem, slab_sem, out_sem,
):
    w, n = lax.axis_index("wide"), lax.axis_index("narrow")
    owner = owner_ref[0]
    funcs = galerkin_ref.shape[1]
    tile = out.shape[0] // TILES

    def rows_of(t):
        return pl.ds(pl.multiple_of(t * tile, tile), tile)

    def column_load(t):
        return pltpu.make_async_copy(column_hbm.at[rows_of(t)], column.at[rows_of(t)], column_sem.at[t])

    def slab_load(t):
        return pltpu.make_async_copy(slab_hbm.at[rows_of(t)], slab.at[rows_of(t)], slab_sem.at[t])

    def out_store(t):
        return pltpu.make_async_copy(out.at[rows_of(t)], out_hbm.at[rows_of(t)], out_sem.at[t])

    for t in range(TILES):
        column_load(t).start()
        slab_load(t).start()
    block[...] = jnp.zeros_like(block)
    for s in range(2):
        for part in range(RING):
            galerkin_ref[s, 12 * part:12 * (part + 1), :] = own_ref[2 * part + s, 0:12, 0:funcs]

    def store(t, factor):
        part = rows_of(t)

        @pl.when(n > owner)
        def _():
            update = lax.dot_general(factor, rows_ref[...], NT, preferred_element_type=F32)
            out[part, :] = (slab[part, :].astype(F32) - update).astype(BF16)

        @pl.when(n == owner)
        def _():
            out[part, :] = factor

        @pl.when(n < owner)
        def _():
            out[part, :] = slab[part, :]

    column_load(0).wait()
    slab_load(0).wait()
    solved = solve(column[0:tile, :], parts_ref[...])
    top = jnp.where(w == owner, lower_ref[...], solved[0:128])
    top = jnp.where(w < owner, 0.0, top)
    factor = jnp.concatenate([top, solved[128:tile]], 0).astype(BF16)
    store(0, factor)

    @pl.when((w == n) & (n > owner))
    def _():
        update = lax.dot_general(factor[0:128], rows_ref[...], NT, preferred_element_type=F32)
        base = slab[0:128, :].astype(F32) + added_of(own_ref, block)
        out[0:128, :] = (base - update).astype(BF16)

    out_store(0).start()

    def body(t, carry):
        column_load(t).wait()
        slab_load(t).wait()
        store(t, solve(column[rows_of(t), :], parts_ref[...]).astype(BF16))
        out_store(t).start()
        return carry

    lax.fori_loop(1, TILES, body, 0)
    for t in range(TILES):
        out_store(t).wait()


def panel_step(owner, own, column, parts, lower, rows, slab, funcs):
    vmem, anyspace = pl.BlockSpec(memory_space=pltpu.VMEM), pl.BlockSpec(memory_space=pl.ANY)
    dma = pltpu.SemaphoreType.DMA
    return pl.pallas_call(
        panel_kernel,
        out_shape=(jax.ShapeDtypeStruct(slab.shape, BF16), jax.ShapeDtypeStruct((2, funcs, funcs), F32)),
        in_specs=[pl.BlockSpec(memory_space=pltpu.SMEM), vmem, vmem, vmem, vmem, anyspace, anyspace],
        out_specs=(anyspace, vmem),
        scratch_shapes=[
            pltpu.VMEM(slab.shape, BF16), pltpu.VMEM(slab.shape, BF16), pltpu.VMEM(slab.shape, BF16),
            pltpu.VMEM((128, 128), F32), dma((TILES,)), dma((TILES,)), dma((TILES,)),
        ],
        compiler_params=pltpu.CompilerParams(vmem_limit_bytes=63 << 20),
        name="panel_step",
    )(owner, own, parts, lower, rows, column, slab)


def on_device(coarse_basis, material_ids, lame_table, coarse_ids, coarse_slab, panel_owner):
    own, column, parts, lower, rows = gather(panel_owner, lame_table, coarse_ids, coarse_basis, material_ids, coarse_slab)
    return panel_step(panel_owner, own, column, parts, lower, rows, coarse_slab, coarse_basis.shape[1])


def solution(mesh):
    return jax.shard_map(
        on_device,
        mesh=mesh,
        in_specs=(
            P("wide", None, None, "narrow", None, None),
            P("wide", "narrow", None, None),
            P(),
            P("wide", None),
            P("wide", "narrow"),
            P(),
        ),
        out_specs=(P("wide", "narrow"), P("wide", None, None)),
        check_vma=False,
    )
```
